128 devices in a mesh: wide: 16 (over y, x), narrow: 8 (over z, core).
Axes of the slice: x: 4, y: 4, z: 4, core: 2. Of those that a mesh axis runs over, the one named last changes fastest.
Arguments:
- hidden: bfloat16 [4096, 2048], P(('wide', 'narrow')), may hold values from -6 to 6
- cotangent: bfloat16 [4096, 2048], P(('wide', 'narrow')), may hold values from -6 to 6
- routes: int32 [4096, 6], P(('wide', 'narrow')), may hold values from 0 to 63, all different within a row; in each aligned block of 32 rows (0 to 31, 32 to 63, ...) at most 6 rows name the same one
- gates: float32 [4096, 6], P(('wide', 'narrow')), may hold values from 0.05 to 1
- offsets: int32 [16], replicated, may hold values from 0 to 15, each once
- w_gate: bfloat16 [128, 2048, 704], P(('wide', 'narrow')), may hold values from -0.125 to 0.125
- w_up: bfloat16 [128, 2048, 704], P(('wide', 'narrow')), may hold values from -0.125 to 0.125
- w_down: bfloat16 [128, 704, 2048], P(('wide', 'narrow')), may hold values from -0.15625 to 0.15625
- w_out: bfloat16 [2048, 2048], P('narrow'), may hold values from -0.125 to 0.125
- latent: bfloat16 [4096, 512], P('wide'), may hold values from -6 to 6
- rope_key: bfloat16 [4096, 64], P('wide'), may hold values from -4 to 4
- q_nope: bfloat16 [4096, 2048], P('wide', 'narrow'), may hold values from -24 to 24
- q_pe: bfloat16 [4096, 1024], P('wide', 'narrow'), may hold values from -100 to 100
- w_uk: bfloat16 [2048, 512], P('narrow'), may hold values from -0.5 to 0.5
- w_uv: bfloat16 [2048, 512], P('narrow'), may hold values from -0.5 to 0.5
Outputs:
- resid_grad: bfloat16 [4096, 2048], P(('wide', 'narrow'))
- grad_q_nope: bfloat16 [4096, 2048], P('wide', 'narrow')
- grad_q_pe: bfloat16 [4096, 1024], P('wide', 'narrow')
- grad_latent: float32 [4096, 512], P(('wide', 'narrow'))
- grad_rope_key: float32 [4096, 64], P(('wide', 'narrow'))
The draws below stay inside these ranges and needn't reach their ends.
Inputs may be any that keep to these rules, and one draw needn't show every extreme that they name: `routes`: each row names 6 different experts; in each aligned block of 32 rows no expert is named by more than 6 rows, and in some blocks one is named by exactly 6. A permutation of the sequence blocks: token i of block b stands at position offsets[b] * 256 + i.
All inputs are finite; a program needn't handle non-finite values.
Results may differ from the reference program's by a relative error of at most 0.028.
Values may be sent and summed in bfloat16 or wider, within the bound.
A program may use at most 128 MiB of HBM per device.

```python
import math
from functools import partial
import jax
import jax.numpy as jnp
import numpy as np
from jax import lax

D = 2048
FFE = 1408
TOPK = 6
HEADS = 16
LATENT = 512
NOPE = 128
ROPE = 64
VDIM = 128
TOK_WIDE = 256
TOKENS = 4096
TOK_DEV = 32
EXPERTS = 64
CAP = 6
N_WIDE = 16


def attention_plan(key):
    base = jax.random.fold_in(key, 9001)
    keys = jax.random.split(base, 8)
    rope = jnp.clip(jax.random.normal(keys[3], (TOKENS, ROPE)), -4.0, 4.0)
    return (rope, keys)


def draw_rope_key(key, part):
    rope, keys = attention_plan(key)
    return rope.astype(jnp.bfloat16)


def draw_q_pe(key, part):
    rope, keys = attention_plan(key)
    drawn = jnp.clip(jax.random.normal(keys[6], (TOKENS, HEADS, ROPE)), -4.0, 4.0)
    values = drawn
    return values.reshape(TOKENS, HEADS * ROPE).astype(jnp.bfloat16)


def draw_q_nope(key, part):
    rope, keys = attention_plan(key)
    values = jnp.clip(jax.random.normal(keys[7], (TOKENS, HEADS, NOPE)), -4.0, 4.0)
    return values.reshape(TOKENS, HEADS * NOPE).astype(jnp.bfloat16)


def level_of(stream_key, shape, cuts, least, high):
    level = 1.0
    for dim, blocks in cuts:
        heights = jax.random.uniform(jax.random.fold_in(jax.random.fold_in(stream_key, 6), dim), (blocks,), jnp.float32, least / len(cuts), high / len(cuts))
        level = level * jnp.repeat(jnp.exp(heights), shape[dim] // blocks).reshape((-1,) + (1,) * (len(shape) - 1 - dim))
    return level


def routed_block(stream_key, own, number, rows, number_of, top, limit, skew):
    order = jax.random.permutation(stream_key, number_of)
    crowded, common = shares(number_of, rows * top, limit, skew, True), shares(number_of, rows * top, limit, skew, False)
    places = jnp.arange(number_of)

    def named(tallies, rotation):
        used = int((tallies > 0).sum())
        fixed = max(1, used // 4)
        moved = fixed + (places - fixed + rotation * (used - fixed)) % max(1, number_of - fixed)
        return jnp.zeros((number_of,), jnp.int32).at[order[jnp.where(places < fixed, places, moved)]].set(jnp.asarray(tallies, jnp.int32))

    tallies = jnp.where(number % 4 == 0, named(crowded, number // 4), named(common, number - number // 4 - 1))
    mixed = jax.random.permutation(jax.random.fold_in(own, 3), number_of)
    giver, receiver = mixed[0:number_of // 2 * 2:2], mixed[1:number_of // 2 * 2:2]
    margin = jnp.minimum(tallies[giver] - 1, limit - tallies[receiver]) // 2
    margin = jnp.where((giver == order[0]) | (receiver == order[0]) | (tallies[receiver] == 0), 0, jnp.maximum(margin, 0))
    moved = jax.random.randint(jax.random.fold_in(own, 4), (number_of // 2,), 0, 1 << 20) % (margin + 1)
    tallies = tallies.at[giver].add(-moved).at[receiver].add(moved)
    items = jnp.searchsorted(jnp.cumsum(tallies), jnp.arange(rows * top), side="right").astype(jnp.int32)
    listing = items.reshape(top, rows).T
    listing = listing[jax.random.permutation(jax.random.fold_in(own, 1), rows)]
    rotation = jax.random.randint(jax.random.fold_in(own, 2), (rows, 1), 0, top)
    return jnp.take_along_axis(listing, (jnp.arange(top)[None, :] + rotation) % top, axis=1)


def shares(number_of, total, reach, lean, full):
    portions = [(1 << 20) // math.isqrt(rank ** lean) + 1 for rank in range(1, number_of + 1)]
    largest = reach if full else min(reach, max(-(-total // number_of), total * portions[0] // sum(portions)))
    least = 1 if total - largest >= number_of - 1 else 0
    holding, rest = [largest] + [least] * (number_of - 1), total - largest - least * (number_of - 1)
    while rest > 0:
        candidates = [i for i in range(1, number_of) if holding[i] < largest] or [i for i in range(1, number_of) if holding[i] < reach]
        mass, left = sum([portions[i] for i in candidates]), rest
        for i in candidates:
            addition = min(reach - holding[i], max(1, left * portions[i] // mass), rest)
            holding[i] = holding[i] + addition
            rest = rest - addition
    return np.array(holding)


def normal_values(stream_key, extent, width, reach, cuts=(), kind=jnp.bfloat16):
    factor_of = level_of(stream_key, extent, cuts, -0.22, 0.18) if cuts else 1.0
    result = jax.random.normal(stream_key, extent, jnp.float32) * width * factor_of
    return jnp.minimum(jnp.maximum(result, -reach), reach).astype(kind)


def setup_inputs(seed: int = 0) -> dict:
    key_of = jax.random.split(jax.random.key(seed), 16)
    hidden = normal_values(key_of[0], (TOKENS, D), 1.0, 6.0, ((0, 128),))
    cotangent = normal_values(key_of[1], (TOKENS, D), 1.0, 6.0, ((0, 128),))
    routes_keys = jax.random.split(jax.random.fold_in(key_of[2], 1), TOKENS // TOK_DEV)
    routes_turns = jax.random.permutation(jax.random.fold_in(key_of[2], 3), TOKENS // TOK_DEV)
    routes = jax.vmap(lambda own, number: routed_block(jax.random.fold_in(key_of[2], 2), own, number, TOK_DEV, EXPERTS, TOPK, CAP, 2))(routes_keys, routes_turns).reshape((TOKENS, TOPK))
    gates = jnp.clip(jnp.exp(math.log(1.0) - 2.9957323 * jax.random.uniform(key_of[3], (TOKENS, TOPK), jnp.float32) ** level_of(key_of[3], (TOKENS, TOPK), ((0, 128),), -0.2, 0.2)), 0.05, 1.0)
    offsets = jax.random.permutation(key_of[4], N_WIDE).astype(jnp.int32)
    w_gate = normal_values(key_of[5], (2 * EXPERTS, D, FFE // 2), D ** -0.5, 0.125, ((0, 128),))
    w_up = normal_values(key_of[6], (2 * EXPERTS, D, FFE // 2), D ** -0.5, 0.125, ((0, 128),))
    w_down = normal_values(key_of[7], (2 * EXPERTS, FFE // 2, D), FFE ** -0.5, 0.15625, ((0, 128),))
    w_out = normal_values(key_of[8], (HEADS * VDIM, D), D ** -0.5, 0.125, ((0, 8),))
    latent = normal_values(key_of[9], (TOKENS, LATENT), 1.0, 6.0, ((0, 16),))
    rope_key = draw_rope_key(jax.random.fold_in(key_of[15], 71), 0)
    q_nope = draw_q_nope(jax.random.fold_in(key_of[15], 71), 0)
    q_pe = draw_q_pe(jax.random.fold_in(key_of[15], 71), 0)
    w_uk = normal_values(key_of[13], (HEADS * NOPE, LATENT), NOPE ** -0.5, 0.5, ((0, 8),))
    w_uv = normal_values(key_of[14], (HEADS * VDIM, LATENT), VDIM ** -0.5, 0.5, ((0, 8),))
    return {"hidden": hidden, "cotangent": cotangent, "routes": routes, "gates": gates, "offsets": offsets, "w_gate": w_gate, "w_up": w_up, "w_down": w_down, "w_out": w_out, "latent": latent, "rope_key": rope_key, "q_nope": q_nope, "q_pe": q_pe, "w_uk": w_uk, "w_uv": w_uv}


def slot_numbers(expert_ids, experts):
    onehot = (expert_ids[:, None] == jnp.arange(experts, dtype=jnp.int32)[None, :]).astype(jnp.int32)
    before = jnp.cumsum(onehot, axis=0) - onehot
    return lax.optimization_barrier(jnp.sum(before * onehot, axis=1)).astype(jnp.int32)

def expert_grad(inputs):
    x_rows, dy_rows, gate_pair, up_pair, down_pair = inputs
    gate_full = jnp.concatenate([gate_pair[0], gate_pair[1]], axis=1)
    up_full = jnp.concatenate([up_pair[0], up_pair[1]], axis=1)
    down_full = jnp.concatenate([down_pair[0], down_pair[1]], axis=0)
    pre_gate = jnp.dot(x_rows, gate_full, preferred_element_type=jnp.float32)
    up_value = jnp.dot(x_rows, up_full, preferred_element_type=jnp.float32)
    grad_hidden = jnp.dot(dy_rows, down_full.T, preferred_element_type=jnp.float32)
    sigmoid_gate = jax.nn.sigmoid(pre_gate)
    grad_gate = (grad_hidden * up_value * sigmoid_gate * (1.0 + pre_gate * (1.0 - sigmoid_gate))).astype(jnp.bfloat16)
    grad_up = (grad_hidden * pre_gate * sigmoid_gate).astype(jnp.bfloat16)
    total = jnp.dot(grad_gate, gate_full.T, preferred_element_type=jnp.float32)
    total = total + jnp.dot(grad_up, up_full.T, preferred_element_type=jnp.float32)
    return total.astype(jnp.bfloat16)

def reference(hidden, cotangent, routes, gates, offsets, w_gate, w_up, w_down, w_out, latent, rope_key, q_nope, q_pe, w_uk, w_uv):
    blocks = TOKENS // TOK_DEV
    block_ids = routes.reshape(blocks, TOK_DEV * TOPK)
    slots = jax.vmap(partial(slot_numbers, experts=EXPERTS))(block_ids).reshape(-1)
    expert_flat = routes.reshape(-1).astype(jnp.int32)
    token_flat = jnp.repeat(jnp.arange(TOKENS, dtype=jnp.int32), TOPK)
    row_flat = (token_flat // TOK_DEV * CAP + slots).astype(jnp.int32)
    weighted = (gates.reshape(-1)[:, None] * cotangent[token_flat].astype(jnp.float32)).astype(jnp.bfloat16)
    zero_rows = jnp.zeros((EXPERTS, blocks * CAP, D), jnp.bfloat16)
    expert_in = zero_rows.at[expert_flat, row_flat].set(hidden[token_flat])
    expert_cot = zero_rows.at[expert_flat, row_flat].set(weighted)
    half_ffe = FFE // 2
    grads = lax.map(expert_grad, (expert_in, expert_cot, w_gate.reshape(EXPERTS, 2, D, half_ffe), w_up.reshape(EXPERTS, 2, D, half_ffe), w_down.reshape(EXPERTS, 2, half_ffe, D)))
    routed = grads[expert_flat, row_flat].astype(jnp.float32).reshape(TOKENS, TOPK, D).sum(axis=1)
    resid_grad = (cotangent.astype(jnp.float32) + routed).astype(jnp.bfloat16)
    score_scale = 1.0 / math.sqrt(NOPE + ROPE)
    grad_out = jnp.dot(resid_grad, w_out.T, preferred_element_type=jnp.float32).astype(jnp.bfloat16)
    local_steps = jnp.arange(TOK_WIDE, dtype=jnp.int32)
    position = (offsets[:, None] * TOK_WIDE + local_steps[None, :]).reshape(-1)
    visible = position[None, :] <= position[:, None]
    q_heads = q_nope.reshape(TOKENS, HEADS, NOPE).transpose(1, 0, 2)
    pe_heads = q_pe.reshape(TOKENS, HEADS, ROPE).transpose(1, 0, 2)
    out_heads = grad_out.reshape(TOKENS, HEADS, VDIM).transpose(1, 0, 2)
    uk_heads = w_uk.reshape(HEADS, NOPE, LATENT)
    uv_heads = w_uv.reshape(HEADS, VDIM, LATENT)

    def one_head(carry, inputs):
        q_one, pe_one, out_one, uk_one, uv_one = inputs
        query_latent = jnp.dot(q_one, uk_one, preferred_element_type=jnp.float32).astype(jnp.bfloat16)
        out_latent = jnp.dot(out_one, uv_one, preferred_element_type=jnp.float32).astype(jnp.bfloat16)
        scores = score_scale * (jnp.dot(query_latent, latent.T, preferred_element_type=jnp.float32) + jnp.dot(pe_one, rope_key.T, preferred_element_type=jnp.float32))
        masked = jnp.where(visible, scores, -1e+30)
        row_max = lax.optimization_barrier(jnp.max(masked, axis=1, keepdims=True))
        log_norm = row_max + jnp.log(lax.optimization_barrier(jnp.sum(jnp.exp(masked - row_max), axis=1, keepdims=True)))
        probs = jnp.exp(masked - log_norm)
        grad_probs = jnp.dot(out_latent, latent.T, preferred_element_type=jnp.float32)
        row_delta = lax.optimization_barrier(jnp.sum(probs * grad_probs, axis=1, keepdims=True))
        grad_scores = (score_scale * probs * (grad_probs - row_delta)).astype(jnp.bfloat16)
        probs_low = probs.astype(jnp.bfloat16)
        grad_qlat = jnp.dot(grad_scores, latent, preferred_element_type=jnp.float32).astype(jnp.bfloat16)
        grad_nope = jnp.dot(grad_qlat, uk_one.T, preferred_element_type=jnp.float32).astype(jnp.bfloat16)
        grad_pe = jnp.dot(grad_scores, rope_key, preferred_element_type=jnp.float32).astype(jnp.bfloat16)
        latent_sum = carry[0] + jnp.dot(probs_low.T, out_latent, preferred_element_type=jnp.float32)
        latent_sum = latent_sum + jnp.dot(grad_scores.T, query_latent, preferred_element_type=jnp.float32)
        rope_sum = carry[1] + jnp.dot(grad_scores.T, pe_one, preferred_element_type=jnp.float32)
        return ((latent_sum, rope_sum), (grad_nope, grad_pe))
    start = (jnp.zeros((TOKENS, LATENT), jnp.float32), jnp.zeros((TOKENS, ROPE), jnp.float32))
    sums, per_head = lax.scan(one_head, start, (q_heads, pe_heads, out_heads, uk_heads, uv_heads))
    grad_q_nope = per_head[0].transpose(1, 0, 2).reshape(TOKENS, HEADS * NOPE)
    grad_q_pe = per_head[1].transpose(1, 0, 2).reshape(TOKENS, HEADS * ROPE)
    return (resid_grad, grad_q_nope, grad_q_pe, sums[0], sums[1])
```

```python
import functools
import math

import jax
import jax.numpy as jnp
from jax import lax
from jax.experimental import pallas as pl
from jax.experimental.pallas import tpu as pltpu
from jax.sharding import PartitionSpec as P

LATENT = 512
NOPE = 128
ROPE = 64
VDIM = 128
MESH = pl.DeviceIdType.MESH
F32 = jnp.float32
BF16 = jnp.bfloat16
NT = (((1,), (1,)), ((), ()))
NN = (((1,), (0,)), ((), ()))
TN = (((0,), (0,)), ((), ()))


def dot(a, b, dims=NN):
    return lax.dot_general(a, b, dims, preferred_element_type=F32)


def iota(shape, dim):
    return lax.broadcasted_iota(jnp.int32, shape, dim)


def place():
    w = lax.axis_index("wide")
    n = lax.axis_index("narrow")
    return w // 4, w % 4, n // 2, n % 2


def selections(rt, gt):
    expert = iota((512, 32), 0) >> 3
    named = jnp.zeros((512, 32), F32)
    weight = jnp.zeros((512, 32), F32)
    for k in range(6):
        hit = expert == rt[k : k + 1, :]
        named = jnp.where(hit, 1.0, named)
        weight = jnp.where(hit, gt[k : k + 1, :], weight)
    earlier = (iota((32, 32), 0) < iota((32, 32), 1)).astype(F32).astype(BF16)
    before = dot(named.astype(BF16), earlier)
    row = iota((512, 32), 0) & 7
    picks = []
    for j in range(3):
        slot = jnp.where(row < 6, row, jnp.where(row == 6, j, 3 + j))
        picks.append(jnp.where(before == slot.astype(F32), named, 0.0))
    return picks, weight, row


def pack_matrix(j):
    q = iota((192, 256), 1)
    r = iota((192, 256), 0)
    s = q & 7
    base = (q >> 3) * 6
    if j < 0:
        return ((s < 6) & (r == base + s)).astype(F32).astype(BF16)
    return ((s >= 6) & (r == base + (s - 6) * 3 + j)).astype(F32).astype(BF16)


def fold_matrix(j):
    q = iota((256, 192), 0)
    r = iota((256, 192), 1)
    s = q & 7
    base = (q >> 3) * 6
    if j < 0:
        return ((s < 6) & (r == base + s)).astype(F32).astype(BF16)
    return ((s >= 6) & (r == base + (s - 6) * 3 + j)).astype(F32).astype(BF16)


def experts_kernel(
    rt, gt, hid, cot, wg, wu, wd,
    own_out, all_out,
    send, recv, back, landed, wgb, wub, wdb, xs, dys, acc, comb,
    lsem, ssem, rsem, wssem, wrsem, bssem, brsem, gsem, hsem, psem,
):
    y, x, z, c = place()
    me = (y * 4 + x) * 4 + z
    partner = (y * 4 + x, z * 2 + 1 - c)
    bar = pltpu.get_barrier_semaphore()

    def peer(k):
        k = (k * 11) % 64
        pw = ((y + k // 16) % 4) * 4 + (x + (k // 4) % 4) % 4
        pz = (z + k % 4) % 4
        return pw * 4 + pz, (pw, pz * 2 + c)

    def greet(k, _):
        pl.semaphore_signal(bar, inc=1, device_id=peer(k)[1], device_id_type=MESH)
        return 0

    lax.fori_loop(1, 64, greet, 0)
    pl.semaphore_signal(bar, inc=1, device_id=partner, device_id_type=MESH)
    loads = [
        pltpu.make_async_copy(src, dst.at[0], lsem.at[i])
        for i, (src, dst) in enumerate(((wg, wgb), (wu, wub), (wd, wdb)))
    ]
    for q in loads:
        q.start()

    picks, weight, row = selections(rt[...], gt[...])
    cot_hi = cot[:, 1024:2048]
    for j in range(3):
        low = jnp.where(row < 6, picks[j], 0.0).astype(BF16)
        high = jnp.where(row < 6, 0.0, picks[j]).astype(BF16)
        if j == 0:
            comb[0] = low
        comb[1 + j] = high
        part = (hid[:, 0:1024], hid[:, 1024:2048], cot[:, 0:1024])[j]
        gate = jnp.sum(picks[j] * weight, axis=1, keepdims=True)
        if j < 2:
            gate = jnp.where(row[:, 0:1] < 6, 1.0, gate)
        val = (dot(low, part) + dot(high, cot_hi)) * gate
        send[:, :, 1024 * j : 1024 * (j + 1)] = val.astype(BF16).reshape(64, 8, 1024)

    pl.semaphore_wait(bar, 64)

    def out_copy(k):
        pc, dev = peer(k)
        return pltpu.make_async_remote_copy(
            send.at[pc], recv.at[me], ssem.at[pc], rsem.at[me], device_id=dev, device_id_type=MESH
        )

    def in_copy(k):
        pc, dev = peer(k)
        return pltpu.make_async_remote_copy(
            send.at[pc], recv.at[pc], ssem.at[pc], rsem.at[pc], device_id=dev, device_id_type=MESH
        )

    def start(k, _):
        out_copy(k).start()
        return 0

    trades = [
        pltpu.make_async_remote_copy(
            src, dst.at[1], wssem.at[i], wrsem.at[i], device_id=partner, device_id_type=MESH
        )
        for i, (src, dst) in enumerate(((wg, wgb), (wu, wub), (wd, wdb)))
    ]
    lax.fori_loop(1, 64, start, 0)
    for q in trades:
        q.start()
    own = pltpu.make_async_copy(send.at[me], recv.at[me], psem.at[0])
    own.start()
    own.wait()

    def finish(k, _):
        q = in_copy(k)
        q.wait_send()
        q.wait_recv()
        return 0

    lax.fori_loop(1, 64, finish, 0)

    for g in range(2):
        got = recv.at[pl.ds(32 * g, 32)]
        rows = pl.ds(192 * g, 192)
        plain = pack_matrix(-1)

        def cols(a, b):
            return got[:, :, a:b].reshape(256, b - a)

        xs[rows, 0:1024] = dot(plain, cols(0, 1024)).astype(BF16)
        xs[rows, 1024:2048] = dot(plain, cols(1024, 2048)).astype(BF16)
        dys[rows, 0:1024] = dot(plain, cols(2048, 3072)).astype(BF16)
        hi = dot(pack_matrix(0), cols(0, 1024))
        hi = hi + dot(pack_matrix(1), cols(1024, 2048))
        hi = hi + dot(pack_matrix(2), cols(2048, 3072))
        dys[rows, 1024:2048] = hi.astype(BF16)

    for h in range(2):
        if h == 0:
            for q in loads:
                q.wait()
        else:
            for q in trades:
                q.wait()
        pre = dot(xs[...], wgb[h], NT)
        up = dot(xs[...], wub[h], NT)
        gh = dot(dys[...], wdb[h], NT)
        s = jax.nn.sigmoid(pre)
        gg = (gh * up * s * (1.0 + pre * (1.0 - s))).astype(BF16)
        gu = (gh * pre * s).astype(BF16)
        for b in range(2):
            cs = slice(1024 * b, 1024 * (b + 1))
            term = dot(gg, wgb[h, :, cs]) + dot(gu, wub[h, :, cs])
            if h == 0:
                acc[:, cs] = term
            else:
                xs[:, cs] = (acc[:, cs] + term).astype(BF16)

    for g in range(2):
        rows = pl.ds(192 * g, 192)
        plain = fold_matrix(-1)
        for j in range(3):
            val = dot(plain, xs[rows, 512 * j : 512 * (j + 1)])
            val = val + dot(fold_matrix(j), xs[rows, 1536:2048])
            back[32 * g : 32 * (g + 1), :, 512 * j : 512 * (j + 1)] = val.astype(BF16).reshape(32, 8, 512)

    def ret_out(k):
        pc, dev = peer(k)
        return pltpu.make_async_remote_copy(
            back.at[pc], landed.at[me], bssem.at[pc], brsem.at[me], device_id=dev, device_id_type=MESH
        )

    def ret_in(k):
        pc, dev = peer(k)
        return pltpu.make_async_remote_copy(
            back.at[pc], landed.at[pc], bssem.at[pc], brsem.at[pc], device_id=dev, device_id_type=MESH
        )

    def ret_start(k, _):
        ret_out(k).start()
        return 0

    lax.fori_loop(1, 64, ret_start, 0)
    own = pltpu.make_async_copy(back.at[me], landed.at[me], psem.at[0])
    own.start()
    own.wait()

    def ret_finish(k, _):
        q = ret_in(k)
        q.wait_send()
        q.wait_recv()
        return 0

    lax.fori_loop(1, 64, ret_finish, 0)

    total = cot[...].astype(F32)
    rest = jnp.zeros((32, 512), F32)
    for j in range(3):
        block = landed[:, :, 512 * j : 512 * (j + 1)].reshape(512, 512)
        cs = slice(512 * j, 512 * (j + 1))
        own_out[:, cs] = (total[:, cs] + dot(comb[0], block, TN)).astype(BF16)
        rest = rest + dot(comb[1 + j], block, TN)
    own_out[:, 1536:2048] = (total[:, 1536:2048] + rest).astype(BF16)
    all_out[z, c] = own_out[...]

    hops = []
    for o in range(1, 4):
        pz = (z + o) % 4
        hops.append(
            pltpu.make_async_remote_copy(
                own_out, all_out.at[z, c], gsem.at[o - 1], hsem.at[o - 1],
                device_id=(y * 4 + x, pz * 2 + c), device_id_type=MESH,
            )
        )
    for q in hops:
        q.start()
    for q in hops:
        q.wait()
    last = pltpu.make_async_remote_copy(
        all_out.at[:, c], all_out.at[:, c], gsem.at[3], hsem.at[3], device_id=partner, device_id_type=MESH
    )
    last.start()
    last.wait()


def experts(rt, gt, hid, cot, wg, wu, wd):
    vm = pl.BlockSpec(memory_space=pltpu.VMEM)
    hbm = pl.BlockSpec(memory_space=pl.ANY)
    dma = pltpu.SemaphoreType.DMA
    half = wg.shape[0]
    return pl.pallas_call(
        experts_kernel,
        out_shape=(
            jax.ShapeDtypeStruct((32, 2048), BF16),
            jax.ShapeDtypeStruct((4, 2, 32, 2048), BF16),
        ),
        in_specs=[vm, vm, vm, vm, hbm, hbm, hbm],
        out_specs=(vm, vm),
        scratch_shapes=[
            pltpu.VMEM((64, 8, 3072), BF16),
            pltpu.VMEM((64, 8, 3072), BF16),
            pltpu.VMEM((64, 8, 1536), BF16),
            pltpu.VMEM((64, 8, 1536), BF16),
            pltpu.VMEM((2, half, 2048), BF16),
            pltpu.VMEM((2, half, 2048), BF16),
            pltpu.VMEM((2, half, 2048), BF16),
            pltpu.VMEM((384, 2048), BF16),
            pltpu.VMEM((384, 2048), BF16),
            pltpu.VMEM((384, 2048), F32),
            pltpu.VMEM((4, 512, 32), BF16),
            dma((3,)), dma((64,)), dma((64,)), dma((3,)), dma((3,)),
            dma((64,)), dma((64,)), dma((4,)), dma((4,)), dma((1,)),
        ],
        compiler_params=pltpu.CompilerParams(
            collective_id=0, has_side_effects=True, vmem_limit_bytes=62 * 1024 * 1024
        ),
        cost_estimate=pl.CostEstimate(flops=11 * 10**9, bytes_accessed=20 * 10**6, transcendentals=10**6),
    )(rt, gt, hid, cot, wg, wu, wd)


ORDERS = ((2, 0, 1), (0, 1, 2), (1, 2, 0))


def scatter_kernel(terms, out, r0, a0, r1, a1, r2, a2, r3, s0, t0, ss, rs):
    y, x, z, c = place()
    coord = (y, x, z)
    partner = (y * 4 + x, z * 2 + 1 - c)

    def device(d, o):
        at = list(coord)
        at[d] = (at[d] + o) % 4
        return (at[0] * 4 + at[1], at[2] * 2 + c)

    bar = pltpu.get_barrier_semaphore()
    pl.semaphore_signal(bar, inc=1, device_id=partner, device_id_type=MESH)
    for d in range(3):
        for o in range(1, 4):
            pl.semaphore_signal(bar, inc=1, device_id=device(d, o), device_id_type=MESH)
    pl.semaphore_wait(bar, 10)
    first = pltpu.make_async_remote_copy(
        terms.at[1 - c], r0, s0, t0, device_id=partner, device_id_type=MESH
    )
    first.start()
    first.wait()

    def add0(i, _):
        at = (i // 16, (i // 4) % 4, i % 4)
        for k in range(3):
            o = ORDERS[k]
            rows = slice(48 * k, 48 * (k + 1))
            val = terms[c, i, rows, :].astype(F32) + r0[i, rows, :].astype(F32)
            a0[k, at[o[0]], at[o[1]], at[o[2]]] = val.astype(BF16)
        return 0

    lax.fori_loop(0, 64, add0, 0)

    def stage(i, src, dst):
        copies = []
        for o in range(1, 4):
            for k in range(3):
                d = ORDERS[k][i]
                copies.append(
                    pltpu.make_async_remote_copy(
                        src.at[k, (coord[d] + o) % 4], dst.at[k, o - 1],
                        ss.at[i, k, o - 1], rs.at[i, k, o - 1],
                        device_id=device(d, o), device_id_type=MESH,
                    )
                )
        for q in copies:
            q.start()
        for q in copies:
            q.wait()

    stage(0, a0, r1)
    for k in range(3):
        mine = coord[ORDERS[k][0]]

        def add1(i, _, k=k, mine=mine):
            val = a0[k, mine, i].astype(F32)
            for o in range(3):
                val = val + r1[k, o, i].astype(F32)
            a1[k, i] = val.astype(BF16)
            return 0

        lax.fori_loop(0, 4, add1, 0)
    stage(1, a1, r2)
    for k in range(3):
        val = a1[k, coord[ORDERS[k][1]]].astype(F32)
        for o in range(3):
            val = val + r2[k, o].astype(F32)
        a2[k] = val.astype(BF16)
    stage(2, a2, r3)
    for k in range(3):
        val = a2[k, coord[ORDERS[k][2]]].astype(F32)
        for o in range(3):
            val = val + r3[k, o].astype(F32)
        out[48 * k : 48 * (k + 1), :] = val


def scatter_sum(terms):
    vm = pl.BlockSpec(memory_space=pltpu.VMEM)
    dma = pltpu.SemaphoreType.DMA
    return pl.pallas_call(
        scatter_kernel,
        out_shape=jax.ShapeDtypeStruct((144, 128), F32),
        in_specs=[vm],
        out_specs=vm,
        scratch_shapes=[
            pltpu.VMEM((64, 144, 128), BF16),
            pltpu.VMEM((3, 4, 4, 4, 48, 128), BF16),
            pltpu.VMEM((3, 3, 4, 4, 48, 128), BF16),
            pltpu.VMEM((3, 4, 4, 48, 128), BF16),
            pltpu.VMEM((3, 3, 4, 48, 128), BF16),
            pltpu.VMEM((3, 4, 48, 128), BF16),
            pltpu.VMEM((3, 3, 48, 128), BF16),
            dma, dma, dma((3, 3, 3)), dma((3, 3, 3)),
        ],
        compiler_params=pltpu.CompilerParams(
            collective_id=1, has_side_effects=True, vmem_limit_bytes=40 * 1024 * 1024
        ),
    )(terms)


def on_device(
    hidden, cotangent, routes, gates, offsets, w_gate, w_up, w_down, w_out,
    latent, rope_key, q_nope, q_pe, w_uk, w_uv,
):
    keys = lax.all_gather(jnp.concatenate([latent, rope_key], axis=1), "wide", axis=0, tiled=True)
    resid_grad, resid_all = experts(
        routes.T, gates.T, hidden, cotangent, w_gate[0].T, w_up[0].T, w_down[0]
    )
    tok_wide = q_nope.shape[0]
    heads = q_nope.shape[1] // NOPE
    scale = 1.0 / math.sqrt(NOPE + ROPE)
    latent_all, rope_all = keys[:, :LATENT], keys[:, LATENT:]
    steps = jnp.arange(tok_wide, dtype=jnp.int32)
    query_pos = offsets[lax.axis_index("wide")] * tok_wide + steps
    key_pos = (offsets[:, None] * tok_wide + steps[None, :]).reshape(-1)
    visible = key_pos[None, :] <= query_pos[:, None]
    k_all = dot(latent_all, w_uk, NT).astype(BF16)
    v_all = dot(latent_all, w_uv, NT).astype(BF16)
    grad_out = dot(resid_all.reshape(tok_wide, -1), w_out, NT).astype(BF16)
    dq, dpe, dks, dvs = [], [], [], []
    rope_term = 0.0
    for h in range(heads):
        hs = slice(NOPE * h, NOPE * (h + 1))
        rs = slice(ROPE * h, ROPE * (h + 1))
        scores = scale * (dot(q_nope[:, hs], k_all[:, hs], NT) + dot(q_pe[:, rs], rope_all, NT))
        masked = jnp.where(visible, scores, -1e30)
        top = jnp.max(masked, axis=1, keepdims=True)
        log_norm = top + jnp.log(jnp.sum(jnp.exp(masked - top), axis=1, keepdims=True))
        probs = jnp.exp(masked - log_norm)
        grad_probs = dot(grad_out[:, hs], v_all[:, hs], NT)
        delta = jnp.sum(probs * grad_probs, axis=1, keepdims=True)
        ds = (scale * probs * (grad_probs - delta)).astype(BF16)
        dq.append(dot(ds, k_all[:, hs]).astype(BF16))
        dpe.append(dot(ds, rope_all).astype(BF16))
        dvs.append(dot(probs.astype(BF16), grad_out[:, hs], TN).astype(BF16))
        dks.append(dot(ds, q_nope[:, hs], TN).astype(BF16))
        rope_term = rope_term + dot(ds, q_pe[:, rs], TN)
    left = jnp.concatenate(dvs + dks, axis=1)
    right = jnp.concatenate([w_uv, w_uk], axis=0)
    latent_term = dot(left, right)
    lat = latent_term.astype(BF16).reshape(64, 2, 32, 4, 128).transpose(1, 0, 3, 2, 4).reshape(2, 64, 128, 128)
    rop = rope_term.astype(BF16).reshape(64, 2, 2, 16, 64).transpose(1, 0, 3, 2, 4).reshape(2, 64, 16, 128)
    mine = scatter_sum(jnp.concatenate([lat, rop], axis=2))
    grad_latent = mine[:128].reshape(4, 32, 128).transpose(1, 0, 2).reshape(32, 512)
    grad_rope = mine[128:].reshape(16, 2, 64).transpose(1, 0, 2).reshape(32, 64)
    return (
        resid_grad,
        jnp.concatenate(dq, axis=1),
        jnp.concatenate(dpe, axis=1),
        grad_latent,
        grad_rope,
    )


def solution(mesh):
    both = ("wide", "narrow")
    return jax.shard_map(
        on_device,
        mesh=mesh,
        in_specs=(
            P(both, None), P(both, None), P(both, None), P(both, None), P(),
            P(both, None, None), P(both, None, None), P(both, None, None),
            P("narrow", None), P("wide", None), P("wide", None),
            P("wide", "narrow"), P("wide", "narrow"), P("narrow", None), P("narrow", None),
        ),
        out_specs=(
            P(both, None), P("wide", "narrow"), P("wide", "narrow"), P(both, None), P(both, None),
        ),
        check_vma=False,
    )
```

```python
import functools
import math

import jax
import jax.numpy as jnp
from jax import lax
from jax.experimental import pallas as pl
from jax.experimental.pallas import tpu as pltpu
from jax.sharding import PartitionSpec as P

LATENT = 512
NOPE = 128
ROPE = 64
VDIM = 128
MESH = pl.DeviceIdType.MESH
F32 = jnp.float32
BF16 = jnp.bfloat16
NT = (((1,), (1,)), ((), ()))
NN = (((1,), (0,)), ((), ()))
TN = (((0,), (0,)), ((), ()))


def dot(a, b, dims=NN):
    return lax.dot_general(a, b, dims, preferred_element_type=F32)


def iota(shape, dim):
    return lax.broadcasted_iota(jnp.int32, shape, dim)


def place():
    w = lax.axis_index("wide")
    n = lax.axis_index("narrow")
    return w // 4, w % 4, n // 2, n % 2


def selections(rt, gt):
    expert = iota((512, 32), 0) >> 3
    named = jnp.zeros((512, 32), F32)
    weight = jnp.zeros((512, 32), F32)
    for k in range(6):
        hit = expert == rt[k : k + 1, :]
        named = jnp.where(hit, 1.0, named)
        weight = jnp.where(hit, gt[k : k + 1, :], weight)
    earlier = (iota((32, 32), 0) < iota((32, 32), 1)).astype(F32).astype(BF16)
    before = dot(named.astype(BF16), earlier)
    row = iota((512, 32), 0) & 7
    picks = []
    for j in range(3):
        slot = jnp.where(row < 6, row, jnp.where(row == 6, j, 3 + j))
        picks.append(jnp.where(before == slot.astype(F32), named, 0.0))
    return picks, weight, row


def pack_matrix(j):
    q = iota((192, 256), 1)
    r = iota((192, 256), 0)
    s = q & 7
    base = (q >> 3) * 6
    if j < 0:
        return ((s < 6) & (r == base + s)).astype(F32).astype(BF16)
    return ((s >= 6) & (r == base + (s - 6) * 3 + j)).astype(F32).astype(BF16)


def fold_matrix(j):
    q = iota((256, 192), 0)
    r = iota((256, 192), 1)
    s = q & 7
    base = (q >> 3) * 6
    if j < 0:
        return ((s < 6) & (r == base + s)).astype(F32).astype(BF16)
    return ((s >= 6) & (r == base + (s - 6) * 3 + j)).astype(F32).astype(BF16)


def experts_kernel(
    rt, gt, hid, cot, wg, wu, wd,
    back, comb,
    send, recv, wgb, wub, wdb, xs, dys, acc,
    lsem, ssem, rsem, wssem, wrsem, psem,
):
    y, x, z, c = place()
    me = (y * 4 + x) * 4 + z
    partner = (y * 4 + x, z * 2 + 1 - c)
    bar = pltpu.get_barrier_semaphore()

    def peer(k):
        k = (k * 11) % 64
        pw = ((y + k // 16) % 4) * 4 + (x + (k // 4) % 4) % 4
        pz = (z + k % 4) % 4
        return pw * 4 + pz, (pw, pz * 2 + c)

    def greet(k, _):
        pl.semaphore_signal(bar, inc=1, device_id=peer(k)[1], device_id_type=MESH)
        return 0

    lax.fori_loop(1, 64, greet, 0)
    pl.semaphore_signal(bar, inc=1, device_id=partner, device_id_type=MESH)
    loads = [
        pltpu.make_async_copy(src, dst.at[0], lsem.at[i])
        for i, (src, dst) in enumerate(((wg, wgb), (wu, wub), (wd, wdb)))
    ]
    for q in loads:
        q.start()

    picks, weight, row = selections(rt[...], gt[...])
    cot_hi = cot[:, 1024:2048]
    for j in range(3):
        low = jnp.where(row < 6, picks[j], 0.0).astype(BF16)
        high = jnp.where(row < 6, 0.0, picks[j]).astype(BF16)
        if j == 0:
            comb[0] = low
        comb[1 + j] = high
        part = (hid[:, 0:1024], hid[:, 1024:2048], cot[:, 0:1024])[j]
        gate = jnp.sum(picks[j] * weight, axis=1, keepdims=True)
        if j < 2:
            gate = jnp.where(row[:, 0:1] < 6, 1.0, gate)
        val = (dot(low, part) + dot(high, cot_hi)) * gate
        send[:, :, 1024 * j : 1024 * (j + 1)] = val.astype(BF16).reshape(64, 8, 1024)

    pl.semaphore_wait(bar, 64)

    def out_copy(k):
        pc, dev = peer(k)
        return pltpu.make_async_remote_copy(
            send.at[pc], recv.at[me], ssem.at[pc], rsem.at[me], device_id=dev, device_id_type=MESH
        )

    def in_copy(k):
        pc, dev = peer(k)
        return pltpu.make_async_remote_copy(
            send.at[pc], recv.at[pc], ssem.at[pc], rsem.at[pc], device_id=dev, device_id_type=MESH
        )

    def start(k, _):
        out_copy(k).start()
        return 0

    trades = [
        pltpu.make_async_remote_copy(
            src, dst.at[1], wssem.at[i], wrsem.at[i], device_id=partner, device_id_type=MESH
        )
        for i, (src, dst) in enumerate(((wg, wgb), (wu, wub), (wd, wdb)))
    ]
    lax.fori_loop(1, 64, start, 0)
    for q in trades:
        q.start()
    own = pltpu.make_async_copy(send.at[me], recv.at[me], psem.at[0])
    own.start()
    own.wait()

    def finish(k, _):
        q = in_copy(k)
        q.wait_send()
        q.wait_recv()
        return 0

    lax.fori_loop(1, 64, finish, 0)

    for g in range(2):
        got = recv.at[pl.ds(32 * g, 32)]
        rows = pl.ds(192 * g, 192)
        plain = pack_matrix(-1)

        def cols(a, b):
            return got[:, :, a:b].reshape(256, b - a)

        xs[rows, 0:1024] = dot(plain, cols(0, 1024)).astype(BF16)
        xs[rows, 1024:2048] = dot(plain, cols(1024, 2048)).astype(BF16)
        dys[rows, 0:1024] = dot(plain, cols(2048, 3072)).astype(BF16)
        hi = dot(pack_matrix(0), cols(0, 1024))
        hi = hi + dot(pack_matrix(1), cols(1024, 2048))
        hi = hi + dot(pack_matrix(2), cols(2048, 3072))
        dys[rows, 1024:2048] = hi.astype(BF16)

    for h in range(2):
        if h == 0:
            for q in loads:
                q.wait()
        else:
            for q in trades:
                q.wait()
        pre = dot(xs[...], wgb[h], NT)
        up = dot(xs[...], wub[h], NT)
        gh = dot(dys[...], wdb[h], NT)
        s = jax.nn.sigmoid(pre)
        gg = (gh * up * s * (1.0 + pre * (1.0 - s))).astype(BF16)
        gu = (gh * pre * s).astype(BF16)
        for b in range(2):
            cs = slice(1024 * b, 1024 * (b + 1))
            term = dot(gg, wgb[h, :, cs]) + dot(gu, wub[h, :, cs])
            if h == 0:
                acc[:, cs] = term
            else:
                xs[:, cs] = (acc[:, cs] + term).astype(BF16)

    for g in range(2):
        rows = pl.ds(192 * g, 192)
        plain = fold_matrix(-1)
        for j in range(3):
            val = dot(plain, xs[rows, 512 * j : 512 * (j + 1)])
            val = val + dot(fold_matrix(j), xs[rows, 1536:2048])
            back[32 * g : 32 * (g + 1), :, 512 * j : 512 * (j + 1)] = val.astype(BF16).reshape(32, 8, 512)


def experts(rt, gt, hid, cot, wg, wu, wd):
    vm = pl.BlockSpec(memory_space=pltpu.VMEM)
    hbm = pl.BlockSpec(memory_space=pl.ANY)
    dma = pltpu.SemaphoreType.DMA
    half = wg.shape[0]
    return pl.pallas_call(
        experts_kernel,
        out_shape=(
            jax.ShapeDtypeStruct((64, 8, 1536), BF16),
            jax.ShapeDtypeStruct((4, 512, 32), BF16),
        ),
        in_specs=[vm, vm, vm, vm, hbm, hbm, hbm],
        out_specs=(vm, vm),
        scratch_shapes=[
            pltpu.VMEM((64, 8, 3072), BF16),
            pltpu.VMEM((64, 8, 3072), BF16),
            pltpu.VMEM((2, half, 2048), BF16),
            pltpu.VMEM((2, half, 2048), BF16),
            pltpu.VMEM((2, half, 2048), BF16),
            pltpu.VMEM((384, 2048), BF16),
            pltpu.VMEM((384, 2048), BF16),
            pltpu.VMEM((384, 2048), F32),
            dma((3,)), dma((64,)), dma((64,)), dma((3,)), dma((3,)), dma((1,)),
        ],
        compiler_params=pltpu.CompilerParams(
            collective_id=0, has_side_effects=True, vmem_limit_bytes=62 * 1024 * 1024
        ),
        cost_estimate=pl.CostEstimate(flops=11 * 10**9, bytes_accessed=20 * 10**6, transcendentals=10**6),
    )(rt, gt, hid, cot, wg, wu, wd)


ORDERS = ((2, 0, 1), (0, 1, 2), (1, 2, 0))
CHUNK = 512
CHUNKS = 8
SCALE = 1.0 / math.sqrt(NOPE + ROPE)


def attention_kernel(
    offs, back, comb, cot, keys, qn, qp, wkv, wout,
    own_out, dq_out, dp_out, out,
    landed, gathered, kc, vx, sc, pr, qc, gx, dd,
    terms, r0, a0, r1, a1, r2, a2, r3,
    bssem, brsem, psem, gsem, hsem, s0, t0, ss, rs,
):
    y, x, z, c = place()
    coord = (y, x, z)
    me = (y * 4 + x) * 4 + z
    partner = (y * 4 + x, z * 2 + 1 - c)

    def peer(k):
        k = (k * 11) % 64
        pw = ((y + k // 16) % 4) * 4 + (x + (k // 4) % 4) % 4
        pz = (z + k % 4) % 4
        return pw * 4 + pz, (pw, pz * 2 + c)

    def device(d, o):
        at = list(coord)
        at[d] = (at[d] + o) % 4
        return (at[0] * 4 + at[1], at[2] * 2 + c)

    bar = pltpu.get_barrier_semaphore()

    def greet(k, _):
        pl.semaphore_signal(bar, inc=1, device_id=peer(k)[1], device_id_type=MESH)
        return 0

    lax.fori_loop(1, 64, greet, 0)
    pl.semaphore_signal(bar, inc=1, device_id=partner, device_id_type=MESH)

    zero = jnp.zeros((256, 64), BF16)
    for h in range(2):
        qc[h, :, 0:128] = qn[:, 128 * h : 128 * (h + 1)]
        qc[h, :, 128:256] = jnp.concatenate([qp[:, 64 * h : 64 * (h + 1)], zero], axis=1)

    pl.semaphore_wait(bar, 64)

    def ret_copy(k, at_me):
        pc, dev = peer(k)
        slot = me if at_me else pc
        return pltpu.make_async_remote_copy(
            back.at[pc], landed.at[slot], bssem.at[pc], brsem.at[slot],
            device_id=dev, device_id_type=MESH,
        )

    def ret_start(k, _):
        ret_copy(k, True).start()
        return 0

    lax.fori_loop(1, 64, ret_start, 0)
    own = pltpu.make_async_copy(back.at[me], landed.at[me], psem)
    own.start()

    ones = (iota((CHUNK, 128), 1) < 2).astype(F32).astype(BF16)
    delta = iota((256, 256), 0) - iota((256, 256), 1)
    here = offs[y * 4 + x]

    def forward(i, tops):
        rows = pl.ds(pl.multiple_of(i * CHUNK, CHUNK), CHUNK)
        kv = dot(keys[rows, 0:512], wkv[...], NT).astype(BF16)
        rope = keys[rows, 512:640]
        new = []
        for h in range(2):
            vx[h, rows, 0:128] = kv[:, 128 * h : 128 * (h + 1)]
            vx[h, rows, 128:256] = ones
            kc[h, rows, 0:128] = kv[:, 256 + 128 * h : 256 + 128 * (h + 1)]
            kc[h, rows, 128:256] = rope
            top = tops[h]
            val = dot(kc[h, rows, :], qc[h], NT)
            for b in range(2):
                limit = (here - offs[2 * i + b]) * 256
                part = jnp.where(delta <= limit, val[256 * b : 256 * (b + 1)], -1e30)
                sc[h, pl.ds(pl.multiple_of(i * CHUNK + 256 * b, 256), 256), :] = part
                top = jnp.maximum(top, jnp.max(part.reshape(32, 8, 256), axis=0))
            new.append(top)
        return tuple(new)

    low = jnp.full((8, 256), -1e30, F32)
    tops = lax.fori_loop(0, CHUNKS, forward, (low, low))
    tops = [jnp.max(t, axis=0, keepdims=True) for t in tops]

    def weigh(i, sums):
        rows = pl.ds(pl.multiple_of(i * CHUNK, CHUNK), CHUNK)
        new = []
        for h in range(2):
            p = jnp.exp(SCALE * (sc[h, rows, :] - tops[h])).astype(BF16)
            pr[h, rows, :] = p
            new.append(sums[h] + dot(p, vx[h, rows, :], TN))
        return tuple(new)

    nil = jnp.zeros((256, 256), F32)
    sums = lax.fori_loop(0, CHUNKS, weigh, (nil, nil))

    own.wait()

    def ret_finish(k, _):
        q = ret_copy(k, False)
        q.wait_send()
        q.wait_recv()
        return 0

    lax.fori_loop(1, 64, ret_finish, 0)

    total = cot[...].astype(F32)
    rest = jnp.zeros((32, 512), F32)
    for j in range(3):
        block = landed[:, :, 512 * j : 512 * (j + 1)].reshape(512, 512)
        cs = slice(512 * j, 512 * (j + 1))
        own_out[:, cs] = (total[:, cs] + dot(comb[0], block, TN)).astype(BF16)
        rest = rest + dot(comb[1 + j], block, TN)
    own_out[:, 1536:2048] = (total[:, 1536:2048] + rest).astype(BF16)
    gathered[z, c] = own_out[...]

    hops = []
    for o in range(1, 4):
        pz = (z + o) % 4
        hops.append(
            pltpu.make_async_remote_copy(
                own_out, gathered.at[z, c], gsem.at[o - 1], hsem.at[o - 1],
                device_id=(y * 4 + x, pz * 2 + c), device_id_type=MESH,
            )
        )
    for q in hops:
        q.start()
    for q in hops:
        q.wait()
    last = pltpu.make_async_remote_copy(
        gathered.at[:, c], gathered.at[:, c], gsem.at[3], hsem.at[3], device_id=partner, device_id_type=MESH
    )
    last.start()
    last.wait()

    go = dot(gathered[...].reshape(256, 2048), wout[...], NT).astype(BF16).astype(F32)
    lane = iota((256, 128), 1)
    for h in range(2):
        inv = 1.0 / sums[h][:, 128:129]
        mean = sums[h][:, 0:128] * inv
        scaled = (go[:, 128 * h : 128 * (h + 1)] * inv).astype(BF16)
        drop = -jnp.sum(scaled.astype(F32) * mean, axis=1, keepdims=True)
        high = drop.astype(BF16).astype(F32)
        extra = jnp.where(lane == 0, high, jnp.where(lane == 1, drop - high, 0.0))
        gx[h, :, 0:128] = scaled
        gx[h, :, 128:256] = extra.astype(BF16)

    def trade(i):
        at = pl.ds(i * 8, 8)
        return pltpu.make_async_remote_copy(
            terms.at[1 - c, at], r0.at[at], s0.at[i], t0.at[i], device_id=partner, device_id_type=MESH
        )

    half = iota((16, 128), 1) < 64

    def backward(i, dqs):
        rows = pl.ds(pl.multiple_of(i * CHUNK, CHUNK), CHUNK)
        new = []
        ropes = 0.0
        for h in range(2):
            p = pr[h, rows, :]
            diff = dot(vx[h, rows, :], gx[h], NT)
            ds = (p.astype(F32) * diff).astype(BF16)
            new.append(dqs[h] + dot(ds, kc[h, rows, :], TN))
            dk = dot(ds, qc[h]) * SCALE
            dd[:, 128 * h : 128 * (h + 1)] = dot(p, gx[h, :, 0:128]).astype(BF16)
            dd[:, 256 + 128 * h : 256 + 128 * (h + 1)] = dk[:, 0:128].astype(BF16)
            ropes = ropes + dk[:, 128:256]
        turned = pltpu.roll(ropes, 64, 1)
        tl = dot(dd[...], wkv[...]).astype(BF16)
        for q in range(16):
            chip = i * 8 + q // 2
            for l in range(4):
                terms[q % 2, chip, 32 * l : 32 * (l + 1), :] = tl[32 * q : 32 * (q + 1), 128 * l : 128 * (l + 1)]
            terms[q % 2, chip, 128:144, :] = jnp.where(
                half, ropes[32 * q : 32 * q + 16], turned[32 * q + 16 : 32 * q + 32]
            ).astype(BF16)
        trade(i).start()
        return tuple(new)

    dqs = lax.fori_loop(0, CHUNKS, backward, (nil, nil))
    for h in range(2):
        val = (dqs[h] * SCALE).astype(BF16)
        dq_out[:, 128 * h : 128 * (h + 1)] = val[:, 0:128]
        dp_out[:, 64 * h : 64 * (h + 1)] = val[:, 128:192]

    def add0(i, _):
        @pl.when(i % 8 == 0)
        def _():
            trade(i // 8).wait()

        at = (i // 16, (i // 4) % 4, i % 4)
        for k in range(3):
            o = ORDERS[k]
            rows = slice(48 * k, 48 * (k + 1))
            val = terms[c, i, rows, :].astype(F32) + r0[i, rows, :].astype(F32)
            a0[k, at[o[0]], at[o[1]], at[o[2]]] = val.astype(BF16)
        return 0

    lax.fori_loop(0, 64, add0, 0)

    def stage(i, src, dst):
        copies = []
        for o in range(1, 4):
            for k in range(3):
                d = ORDERS[k][i]
                copies.append(
                    pltpu.make_async_remote_copy(
                        src.at[k, (coord[d] + o) % 4], dst.at[k, o - 1],
                        ss.at[i, k, o - 1], rs.at[i, k, o - 1],
                        device_id=device(d, o), device_id_type=MESH,
                    )
                )
        for q in copies:
            q.start()
        for q in copies:
            q.wait()

    stage(0, a0, r1)
    for k in range(3):
        mine = coord[ORDERS[k][0]]

        def add1(i, _, k=k, mine=mine):
            val = a0[k, mine, i].astype(F32)
            for o in range(3):
                val = val + r1[k, o, i].astype(F32)
            a1[k, i] = val.astype(BF16)
            return 0

        lax.fori_loop(0, 4, add1, 0)
    stage(1, a1, r2)
    for k in range(3):
        val = a1[k, coord[ORDERS[k][1]]].astype(F32)
        for o in range(3):
            val = val + r2[k, o].astype(F32)
        a2[k] = val.astype(BF16)
    stage(2, a2, r3)
    for k in range(3):
        val = a2[k, coord[ORDERS[k][2]]].astype(F32)
        for o in range(3):
            val = val + r3[k, o].astype(F32)
        out[48 * k : 48 * (k + 1), :] = val


def attention(offs, back, comb, cot, keys, qn, qp, wkv, wout):
    vm = pl.BlockSpec(memory_space=pltpu.VMEM)
    sm = pl.BlockSpec(memory_space=pltpu.SMEM)
    dma = pltpu.SemaphoreType.DMA
    return pl.pallas_call(
        attention_kernel,
        out_shape=(
            jax.ShapeDtypeStruct((32, 2048), BF16),
            jax.ShapeDtypeStruct((256, 256), BF16),
            jax.ShapeDtypeStruct((256, 128), BF16),
            jax.ShapeDtypeStruct((144, 128), F32),
        ),
        in_specs=[sm, vm, vm, vm, vm, vm, vm, vm, vm],
        out_specs=(vm, vm, vm, vm),
        scratch_shapes=[
            pltpu.VMEM((64, 8, 1536), BF16),
            pltpu.VMEM((4, 2, 32, 2048), BF16),
            pltpu.VMEM((2, 4096, 256), BF16),
            pltpu.VMEM((2, 4096, 256), BF16),
            pltpu.VMEM((2, 4096, 256), F32),
            pltpu.VMEM((2, 4096, 256), BF16),
            pltpu.VMEM((2, 256, 256), BF16),
            pltpu.VMEM((2, 256, 256), BF16),
            pltpu.VMEM((CHUNK, 512), BF16),
            pltpu.VMEM((2, 64, 144, 128), BF16),
            pltpu.VMEM((64, 144, 128), BF16),
            pltpu.VMEM((3, 4, 4, 4, 48, 128), BF16),
            pltpu.VMEM((3, 3, 4, 4, 48, 128), BF16),
            pltpu.VMEM((3, 4, 4, 48, 128), BF16),
            pltpu.VMEM((3, 3, 4, 48, 128), BF16),
            pltpu.VMEM((3, 4, 48, 128), BF16),
            pltpu.VMEM((3, 3, 48, 128), BF16),
            dma((64,)), dma((64,)), dma, dma((4,)), dma((4,)),
            dma((CHUNKS,)), dma((CHUNKS,)), dma((3, 3, 3)), dma((3, 3, 3)),
        ],
        compiler_params=pltpu.CompilerParams(
            collective_id=1, has_side_effects=True, vmem_limit_bytes=62 * 1024 * 1024
        ),
        cost_estimate=pl.CostEstimate(flops=11 * 10**9, bytes_accessed=10 * 10**6, transcendentals=2 * 10**6),
    )(offs, back, comb, cot, keys, qn, qp, wkv, wout)


def on_device(
    hidden, cotangent, routes, gates, offsets, w_gate, w_up, w_down, w_out,
    latent, rope_key, q_nope, q_pe, w_uk, w_uv,
):
    blank = jnp.zeros_like(rope_key)
    keys = lax.all_gather(
        jnp.concatenate([latent, rope_key, blank], axis=1), "wide", axis=0, tiled=True
    )
    back, comb = experts(
        routes.T, gates.T, hidden, cotangent, w_gate[0].T, w_up[0].T, w_down[0]
    )
    resid_grad, dq, dpe, mine = attention(
        offsets, back, comb, cotangent, keys, q_nope, q_pe,
        jnp.concatenate([w_uv, w_uk], axis=0), w_out,
    )
    grad_latent = mine[:128].reshape(4, 32, 128).transpose(1, 0, 2).reshape(32, 512)
    grad_rope = mine[128:].reshape(16, 2, 64).transpose(1, 0, 2).reshape(32, 64)
    return (resid_grad, dq, dpe, grad_latent, grad_rope)


def solution(mesh):
    both = ("wide", "narrow")
    return jax.shard_map(
        on_device,
        mesh=mesh,
        in_specs=(
            P(both, None), P(both, None), P(both, None), P(both, None), P(),
            P(both, None, None), P(both, None, None), P(both, None, None),
            P("narrow", None), P("wide", None), P("wide", None),
            P("wide", "narrow"), P("wide", "narrow"), P("narrow", None), P("narrow", None),
        ),
        out_specs=(
            P(both, None), P("wide", "narrow"), P("wide", "narrow"), P(both, None), P(both, None),
        ),
        check_vma=False,
    )
```

```python
import functools
import math

import jax
import jax.numpy as jnp
from jax import lax
from jax.experimental import pallas as pl
from jax.experimental.pallas import tpu as pltpu
from jax.sharding import PartitionSpec as P

LATENT = 512
NOPE = 128
ROPE = 64
VDIM = 128
MESH = pl.DeviceIdType.MESH
F32 = jnp.float32
BF16 = jnp.bfloat16
NT = (((1,), (1,)), ((), ()))
NN = (((1,), (0,)), ((), ()))
TN = (((0,), (0,)), ((), ()))


def dot(a, b, dims=NN):
    return lax.dot_general(a, b, dims, preferred_element_type=F32)


def iota(shape, dim):
    return lax.broadcasted_iota(jnp.int32, shape, dim)


def place():
    w = lax.axis_index("wide")
    n = lax.axis_index("narrow")
    return w // 4, w % 4, n // 2, n % 2


def selections(rt, gt):
    expert = iota((512, 32), 0) >> 3
    named = jnp.zeros((512, 32), F32)
    weight = jnp.zeros((512, 32), F32)
    for k in range(6):
        hit = expert == rt[k : k + 1, :]
        named = jnp.where(hit, 1.0, named)
        weight = jnp.where(hit, gt[k : k + 1, :], weight)
    earlier = (iota((32, 32), 0) < iota((32, 32), 1)).astype(F32).astype(BF16)
    before = dot(named.astype(BF16), earlier)
    row = iota((512, 32), 0) & 7
    picks = []
    for j in range(3):
        slot = jnp.where(row < 6, row, jnp.where(row == 6, j, 3 + j))
        picks.append(jnp.where(before == slot.astype(F32), named, 0.0))
    return picks, weight, row


def pack_matrix(j):
    q = iota((192, 256), 1)
    r = iota((192, 256), 0)
    s = q & 7
    base = (q >> 3) * 6
    if j < 0:
        return ((s < 6) & (r == base + s)).astype(F32).astype(BF16)
    return ((s >= 6) & (r == base + (s - 6) * 3 + j)).astype(F32).astype(BF16)


def fold_matrix(j):
    q = iota((256, 192), 0)
    r = iota((256, 192), 1)
    s = q & 7
    base = (q >> 3) * 6
    if j < 0:
        return ((s < 6) & (r == base + s)).astype(F32).astype(BF16)
    return ((s >= 6) & (r == base + (s - 6) * 3 + j)).astype(F32).astype(BF16)


ORDERS = ((2, 0, 1), (0, 1, 2), (1, 2, 0))
CHUNK = 512
CHUNKS = 8
SCALE = 1.0 / math.sqrt(NOPE + ROPE)


def layer_kernel(
    offs, rt, gt, hid, cot, lat, rope, qn, qp, wuv, wuk, wout, wg, wu, wd,
    own_out, dq_out, dp_out, out,
    send, recv, wgb, wub, wdb, back, landed, keys, gathered, comb, xs, dys, sc,
    wkv, qc, gx, dd, terms, r0, r1, ry, a1, r2, a2, r3,
    lsem, psem, ssem, rsem, wssem, wrsem, bssem, brsem, asem, bsem, gsem, hsem,
    s0, t0, s1, t1, sy, ty, ss, rs,
):
    y, x, z, c = place()
    coord = (y, x, z)
    me = (y * 4 + x) * 4 + z
    partner = (y * 4 + x, z * 2 + 1 - c)

    def peer(k, sign=1):
        k = (k * 11) % 64
        pw = ((y + 4 + sign * (k // 16)) % 4) * 4 + (x + 4 + sign * ((k // 4) % 4)) % 4
        pz = (z + 4 + sign * (k % 4)) % 4
        return pw * 4 + pz, (pw, pz * 2 + c)

    def device(d, o):
        at = list(coord)
        at[d] = (at[d] + o) % 4
        return (at[0] * 4 + at[1], at[2] * 2 + c)

    def remote(src, dst, a, b, dev):
        return pltpu.make_async_remote_copy(
            src_ref=src, dst_ref=dst, send_sem=a, recv_sem=b, device_id=dev, device_id_type=MESH
        )

    bar = pltpu.get_barrier_semaphore()

    def greet(k, _):
        pl.semaphore_signal(bar, inc=1, device_id=peer(k)[1], device_id_type=MESH)
        return 0

    lax.fori_loop(1, 64, greet, 0)
    pl.semaphore_signal(bar, inc=1, device_id=partner, device_id_type=MESH)
    weights = ((wg, wgb), (wu, wub), (wd, wdb))
    loads = [pltpu.make_async_copy(a, b.at[0], lsem.at[i]) for i, (a, b) in enumerate(weights)]
    for q in loads:
        q.start()

    picks, weight, row = selections(rt[...], gt[...])
    cot_hi = cot[:, 1024:2048]
    for j in range(3):
        low = jnp.where(row < 6, picks[j], 0.0).astype(BF16)
        high = jnp.where(row < 6, 0.0, picks[j]).astype(BF16)
        if j == 0:
            comb[0] = low
        comb[1 + j] = high
        part = (hid[:, 0:1024], hid[:, 1024:2048], cot[:, 0:1024])[j]
        gate = jnp.sum(picks[j] * weight, axis=1, keepdims=True)
        if j < 2:
            gate = jnp.where(row[:, 0:1] < 6, 1.0, gate)
        val = (dot(low, part) + dot(high, cot_hi)) * gate
        send[:, :, 1024 * j : 1024 * (j + 1)] = val.astype(BF16).reshape(64, 8, 1024)
    zero = jnp.zeros((256, 64), BF16)
    keys[y, x, :, :, :, 0:512] = lat[...].reshape(2, 2, 64, 512)
    keys[y, x, :, :, :, 512:640] = jnp.concatenate([rope[...], zero], axis=1).reshape(2, 2, 64, 128)

    pl.semaphore_wait(bar, 64)

    def start(k, _):
        pc, dev = peer(k)
        remote(send.at[pc], recv.at[k], ssem.at[k], rsem.at[k], dev).start()
        return 0

    trades = [
        remote(a, b.at[1], wssem.at[i], wrsem.at[i], partner) for i, (a, b) in enumerate(weights)
    ]
    spread = []
    for k, d in ((0, 1), (1, 0)):
        for o in range(1, 4):
            at = keys.at[y, x, c, k]
            spread.append(remote(at, at, asem.at[0, k, o - 1], bsem.at[0, k, o - 1], device(d, o)))
    own = pltpu.make_async_copy(send.at[me], recv.at[0], psem)
    own.start()
    lax.fori_loop(1, 64, start, 0)
    for q in trades:
        q.start()
    for q in spread:
        q.start()
    for h in range(2):
        qc[h, :, 0:128] = qn[:, 128 * h : 128 * (h + 1)]
        qc[h, :, 128:256] = jnp.concatenate([qp[:, 64 * h : 64 * (h + 1)], zero], axis=1)
    wkv[0:256, :] = wuv[...]
    wkv[256:512, :] = wuk[...]
    own.wait()

    def arrive(k, _):
        remote(send.at[0], recv.at[k], ssem.at[k], rsem.at[k], partner).wait_recv()
        return 0

    def ret_start(k, _):
        remote(back.at[k], landed.at[me], bssem.at[k], brsem.at[me], peer(k, -1)[1]).start()
        return 0

    widen = []
    for k, d in ((0, 0), (1, 1)):
        for o in range(1, 4):
            at = keys.at[y, :, c, 0] if k == 0 else keys.at[:, x, c, 1]
            widen.append(remote(at, at, asem.at[1, k, o - 1], bsem.at[1, k, o - 1], device(d, o)))
    mirror = remote(keys.at[:, :, c], keys.at[:, :, c], gsem.at[4], hsem.at[4], partner)

    for g in range(2):
        lax.fori_loop(max(1, 32 * g), 32 * (g + 1), arrive, 0)
        plain = pack_matrix(-1)

        def cols(a, b, g=g):
            return recv[32 * g : 32 * (g + 1), :, a:b].reshape(256, b - a)

        xs[:, 0:1024] = dot(plain, cols(0, 1024)).astype(BF16)
        xs[:, 1024:2048] = dot(plain, cols(1024, 2048)).astype(BF16)
        dys[:, 0:1024] = dot(plain, cols(2048, 3072)).astype(BF16)
        hi = dot(pack_matrix(0), cols(0, 1024))
        hi = hi + dot(pack_matrix(1), cols(1024, 2048))
        hi = hi + dot(pack_matrix(2), cols(2048, 3072))
        dys[:, 1024:2048] = hi.astype(BF16)
        if g == 0:
            for q in loads:
                q.wait()
        for h in range(2):
            if g == 0 and h == 1:
                for q in trades:
                    q.wait()
            if g == 1 and h == 1:
                for q in widen:
                    q.wait()
                mirror.start()
            pre = dot(xs[...], wgb[h], NT)
            up = dot(xs[...], wub[h], NT)
            gh = dot(dys[...], wdb[h], NT)
            s = jax.nn.sigmoid(pre)
            gg = (gh * up * s * (1.0 + pre * (1.0 - s))).astype(BF16)
            gu = (gh * pre * s).astype(BF16)
            for b in range(2):
                cs = slice(1024 * b, 1024 * (b + 1))
                term = dot(gg, wgb[h, :, cs]) + dot(gu, wub[h, :, cs])
                if h == 0:
                    sc[0, 0:192, cs] = term
                else:
                    xs[:, cs] = (sc[0, 0:192, cs] + term).astype(BF16)
        plain = fold_matrix(-1)
        for j in range(3):
            val = dot(plain, xs[:, 512 * j : 512 * (j + 1)])
            val = val + dot(fold_matrix(j), xs[:, 1536:2048])
            back[32 * g : 32 * (g + 1), :, 512 * j : 512 * (j + 1)] = val.astype(BF16).reshape(32, 8, 512)
        if g == 0:
            for q in spread:
                q.wait()
            for q in widen:
                q.start()
            own = pltpu.make_async_copy(back.at[0], landed.at[me], psem)
            own.start()
        lax.fori_loop(max(1, 32 * g), 32 * (g + 1), ret_start, 0)

    mirror.wait()
    ones = (iota((CHUNK, 128), 1) < 2).astype(F32).astype(BF16)
    delta = iota((256, 256), 0) - iota((256, 256), 1)
    here = offs[y * 4 + x]

    def block(i):
        return slice(0, CHUNK), pl.ds(pl.multiple_of(i * 256, 256), 256)

    def forward(i, tops):
        sub, at = block(i)
        chunk = keys[i // 2, pl.ds((i % 2) * 2, 2)].reshape(CHUNK, 640)
        kv = dot(chunk[:, 0:512], wkv[...], NT).astype(BF16)
        new = []
        for h in range(2):
            vx = jnp.concatenate([kv[:, 128 * h : 128 * (h + 1)], ones], axis=1)
            kc = jnp.concatenate([kv[:, 256 + 128 * h : 256 + 128 * (h + 1)], chunk[:, 512:640]], axis=1)
            wdb[h, sub, at] = vx
            wub[h, sub, at] = kc
            top = tops[h]
            val = dot(kc, qc[h], NT)
            for b in range(2):
                limit = (here - offs[2 * i + b]) * 256
                part = jnp.where(delta <= limit, val[256 * b : 256 * (b + 1)], -1e30)
                sc[h, 256 * b : 256 * (b + 1), at] = part
                top = jnp.maximum(top, jnp.max(part.reshape(32, 8, 256), axis=0))
            new.append(top)
        return tuple(new)

    least = jnp.full((8, 256), -1e30, F32)
    tops = lax.fori_loop(0, CHUNKS, forward, (least, least))
    tops = [jnp.max(t, axis=0, keepdims=True) for t in tops]

    def weigh(i, sums):
        sub, at = block(i)
        new = []
        for h in range(2):
            p = jnp.exp(SCALE * (sc[h, sub, at] - tops[h])).astype(BF16)
            wgb[h, sub, at] = p
            new.append(sums[h] + dot(p, wdb[h, sub, at], TN))
        return tuple(new)

    nil = jnp.zeros((256, 256), F32)
    sums = lax.fori_loop(0, CHUNKS, weigh, (nil, nil))

    own.wait()

    def ret_finish(k, _):
        pc = peer(k)[0]
        remote(send.at[0], recv.at[k], ssem.at[k], rsem.at[k], partner).wait_send()
        q = remote(back.at[k], landed.at[pc], bssem.at[k], brsem.at[pc], partner)
        q.wait_send()
        q.wait_recv()
        return 0

    lax.fori_loop(1, 64, ret_finish, 0)

    total = cot[...].astype(F32)
    rest = jnp.zeros((32, 512), F32)
    for j in range(3):
        part = landed[:, :, 512 * j : 512 * (j + 1)].reshape(512, 512)
        cs = slice(512 * j, 512 * (j + 1))
        own_out[:, cs] = (total[:, cs] + dot(comb[0], part, TN)).astype(BF16)
        rest = rest + dot(comb[1 + j], part, TN)
    own_out[:, 1536:2048] = (total[:, 1536:2048] + rest).astype(BF16)
    gathered[z, c] = own_out[...]
    hops = [
        remote(own_out, gathered.at[z, c], gsem.at[o - 1], hsem.at[o - 1], device(2, o))
        for o in range(1, 4)
    ]
    for q in hops:
        q.start()
    for q in hops:
        q.wait()
    last = remote(gathered.at[:, c], gathered.at[:, c], gsem.at[3], hsem.at[3], partner)
    last.start()
    last.wait()

    go = dot(gathered[...].reshape(256, 2048), wout[...], NT).astype(BF16).astype(F32)
    lane = iota((256, 128), 1)
    for h in range(2):
        inv = 1.0 / sums[h][:, 128:129]
        mean = sums[h][:, 0:128] * inv
        scaled = (go[:, 128 * h : 128 * (h + 1)] * inv).astype(BF16)
        drop = -jnp.sum(scaled.astype(F32) * mean, axis=1, keepdims=True)
        high = drop.astype(BF16).astype(F32)
        extra = jnp.where(lane == 0, high, jnp.where(lane == 1, drop - high, 0.0))
        gx[h, :, 0:128] = scaled
        gx[h, :, 128:256] = extra.astype(BF16)

    def trade(r):
        g = (y + 1 + r) % 4
        return remote(terms.at[1 - c, g], r0.at[g], s0.at[r], t0.at[r], partner)

    left = iota((16, 128), 1) < 64

    def backward(i, dqs):
        sub, at = block(i)
        new = []
        ropes = 0.0
        for h in range(2):
            p = wgb[h, sub, at]
            diff = dot(wdb[h, sub, at], gx[h], NT)
            ds = (p.astype(F32) * diff).astype(BF16)
            new.append(dqs[h] + dot(ds, wub[h, sub, at], TN))
            dk = dot(ds, qc[h]) * SCALE
            dd[:, 128 * h : 128 * (h + 1)] = dot(p, gx[h, :, 0:128]).astype(BF16)
            dd[:, 256 + 128 * h : 256 + 128 * (h + 1)] = dk[:, 0:128].astype(BF16)
            ropes = ropes + dk[:, 128:256]
        turned = pltpu.roll(ropes, 64, 1)
        tl = dot(dd[...], wkv[...]).astype(BF16)
        for q in range(16):
            e, f, m = i // 2, (i % 2) * 2 + q // 8, (q // 2) % 4
            for l in range(4):
                terms[q % 2, e, f, m, 32 * l : 32 * (l + 1), :] = tl[32 * q : 32 * (q + 1), 128 * l : 128 * (l + 1)]
            terms[q % 2, e, f, m, 128:144, :] = jnp.where(
                left, ropes[32 * q : 32 * q + 16], turned[32 * q + 16 : 32 * q + 32]
            ).astype(BF16)
        return tuple(new)

    def near(r, k, o):
        g = (y + 1 + r) % 4
        d = ORDERS[k][0]
        rows = pl.ds(48 * k, 48)
        to = (coord[d] + o) % 4
        src = terms.at[c, g, :, to, rows] if k == 0 else terms.at[c, g, to, :, rows]
        i = k // 2
        return remote(src, r1.at[i, o - 1, g], s1.at[i, o - 1, r], t1.at[i, o - 1, r], device(d, o))

    def far(r):
        g = (y + 1 + r) % 4
        pz = z * 2 + c
        return remote(terms.at[c, g, :, :, pl.ds(48, 48)], ry.at[r], sy.at[r], ty.at[r], (g * 4 + x, pz))

    def settle(r):
        trade(r).wait()
        g = (y + 1 + r) % 4

        def add(i, _):
            a, b = i // 4, i % 4
            val = terms[c, g, a, b].astype(F32) + r0[g, a, b].astype(F32)
            terms[c, g, a, b] = val.astype(BF16)
            return 0

        lax.fori_loop(0, 16, add, 0)
        for o in range(1, 4):
            near(r, 0, o).start()
            near(r, 2, o).start()

        @pl.when(r < 3)
        def _():
            far(r).start()

    def quarter(r, dqs):
        i = ((y + 1 + r) % 4) * 2
        dqs = lax.fori_loop(i, i + 2, backward, dqs)
        trade(r).start()

        @pl.when(r > 0)
        def _():
            settle(r - 1)

        return dqs

    dqs = lax.fori_loop(0, 4, quarter, (nil, nil))
    for h in range(2):
        val = (dqs[h] * SCALE).astype(BF16)
        dq_out[:, 128 * h : 128 * (h + 1)] = val[:, 0:128]
        dp_out[:, 64 * h : 64 * (h + 1)] = val[:, 128:192]
    settle(3)

    def close(r, _):
        for o in range(1, 4):
            near(r, 0, o).wait()
            near(r, 2, o).wait()

        @pl.when(r < 3)
        def _():
            far(r).wait()

        return 0

    lax.fori_loop(0, 4, close, 0)

    def add1(i, _):
        a, b = i // 4, i % 4
        val = terms[c, a, b, z, 0:48].astype(F32)
        for o in range(3):
            val = val + r1[0, o, a, b].astype(F32)
        a1[0, a, b] = val.astype(BF16)
        val = terms[c, y, a, b, 48:96].astype(F32)
        for o in range(3):
            val = val + ry[o, a, b].astype(F32)
        a1[1, a, b] = val.astype(BF16)
        val = terms[c, a, x, b, 96:144].astype(F32)
        for o in range(3):
            val = val + r1[1, o, a, b].astype(F32)
        a1[2, b, a] = val.astype(BF16)
        return 0

    lax.fori_loop(0, 16, add1, 0)

    def stage(i, src, dst):
        copies = []
        for o in range(1, 4):
            for k in range(3):
                d = ORDERS[k][i]
                copies.append(
                    remote(
                        src.at[k, (coord[d] + o) % 4], dst.at[k, o - 1],
                        ss.at[i - 1, k, o - 1], rs.at[i - 1, k, o - 1], device(d, o),
                    )
                )
        for q in copies:
            q.start()
        for q in copies:
            q.wait()

    stage(1, a1, r2)
    for k in range(3):
        val = a1[k, coord[ORDERS[k][1]]].astype(F32)
        for o in range(3):
            val = val + r2[k, o].astype(F32)
        a2[k] = val.astype(BF16)
    stage(2, a2, r3)
    for k in range(3):
        val = a2[k, coord[ORDERS[k][2]]].astype(F32)
        for o in range(3):
            val = val + r3[k, o].astype(F32)
        out[48 * k : 48 * (k + 1), :] = val


def layer(*args):
    vm = pl.BlockSpec(memory_space=pltpu.VMEM)
    sm = pl.BlockSpec(memory_space=pltpu.SMEM)
    hbm = pl.BlockSpec(memory_space=pl.ANY)
    dma = pltpu.SemaphoreType.DMA
    half = args[-1].shape[0]

    def room(*shape, dtype=BF16):
        return pltpu.VMEM(shape, dtype)

    return pl.pallas_call(
        layer_kernel,
        out_shape=(
            jax.ShapeDtypeStruct((32, 2048), BF16),
            jax.ShapeDtypeStruct((256, 256), BF16),
            jax.ShapeDtypeStruct((256, 128), BF16),
            jax.ShapeDtypeStruct((144, 128), F32),
        ),
        in_specs=[sm] + [vm] * 11 + [hbm] * 3,
        out_specs=(vm, vm, vm, vm),
        scratch_shapes=[
            room(64, 8, 3072), room(64, 8, 3072),
            room(2, half, 2048), room(2, half, 2048), room(2, half, 2048),
            room(64, 8, 1536), room(64, 8, 1536),
            room(4, 4, 2, 2, 64, 640), room(4, 2, 32, 2048), room(4, 512, 32),
            room(192, 2048), room(192, 2048), room(2, 512, 2048, dtype=F32),
            room(512, 512), room(2, 256, 256), room(2, 256, 256), room(CHUNK, 512),
            room(2, 4, 4, 4, 144, 128), room(4, 4, 4, 144, 128),
            room(2, 3, 4, 4, 48, 128), room(3, 4, 4, 48, 128),
            room(3, 4, 4, 48, 128), room(3, 3, 4, 48, 128),
            room(3, 4, 48, 128), room(3, 3, 48, 128),
            dma((3,)), dma, dma((64,)), dma((64,)), dma((3,)), dma((3,)),
            dma((64,)), dma((64,)), dma((2, 2, 3)), dma((2, 2, 3)), dma((5,)), dma((5,)),
            dma((4,)), dma((4,)), dma((2, 3, 4)), dma((2, 3, 4)), dma((3,)), dma((3,)),
            dma((2, 3, 3)), dma((2, 3, 3)),
        ],
        compiler_params=pltpu.CompilerParams(
            collective_id=0, has_side_effects=True, vmem_limit_bytes=67043328
        ),
        cost_estimate=pl.CostEstimate(flops=22 * 10**9, bytes_accessed=20 * 10**6, transcendentals=3 * 10**6),
    )(*args)


def on_device(
    hidden, cotangent, routes, gates, offsets, w_gate, w_up, w_down, w_out,
    latent, rope_key, q_nope, q_pe, w_uk, w_uv,
):
    resid_grad, dq, dpe, mine = layer(
        offsets, routes.T, gates.T, hidden, cotangent, latent, rope_key, q_nope, q_pe,
        w_uv, w_uk, w_out, w_gate[0].T, w_up[0].T, w_down[0],
    )
    grad_latent = mine[:128].reshape(4, 32, 128).transpose(1, 0, 2).reshape(32, 512)
    grad_rope = mine[128:].reshape(16, 2, 64).transpose(1, 0, 2).reshape(32, 64)
    return (resid_grad, dq, dpe, grad_latent, grad_rope)


def solution(mesh):
    both = ("wide", "narrow")
    return jax.shard_map(
        on_device,
        mesh=mesh,
        in_specs=(
            P(both, None), P(both, None), P(both, None), P(both, None), P(),
            P(both, None, None), P(both, None, None), P(both, None, None),
            P("narrow", None), P("wide", None), P("wide", None),
            P("wide", "narrow"), P("wide", "narrow"), P("narrow", None), P("narrow", None),
        ),
        out_specs=(
            P(both, None), P("wide", "narrow"), P("wide", "narrow"), P(both, None), P(both, None),
        ),
        check_vma=False,
    )
```

```python
import functools
import math

import jax
import jax.numpy as jnp
from jax import lax
from jax.experimental import pallas as pl
from jax.experimental.pallas import tpu as pltpu
from jax.sharding import PartitionSpec as P

LATENT = 512
NOPE = 128
ROPE = 64
VDIM = 128
MESH = pl.DeviceIdType.MESH
F32 = jnp.float32
BF16 = jnp.bfloat16
NT = (((1,), (1,)), ((), ()))
NN = (((1,), (0,)), ((), ()))
TN = (((0,), (0,)), ((), ()))


def dot(a, b, dims=NN):
    return lax.dot_general(a, b, dims, preferred_element_type=F32)


def iota(shape, dim):
    return lax.broadcasted_iota(jnp.int32, shape, dim)


def place():
    w = lax.axis_index("wide")
    n = lax.axis_index("narrow")
    return w // 4, w % 4, n // 2, n % 2


def selections(rt, gt):
    expert = iota((512, 32), 0) >> 3
    named = jnp.zeros((512, 32), F32)
    weight = jnp.zeros((512, 32), F32)
    for k in range(6):
        hit = expert == rt[k : k + 1, :]
        named = jnp.where(hit, 1.0, named)
        weight = jnp.where(hit, gt[k : k + 1, :], weight)
    earlier = (iota((32, 32), 0) < iota((32, 32), 1)).astype(F32).astype(BF16)
    before = dot(named.astype(BF16), earlier)
    row = iota((512, 32), 0) & 7
    picks = []
    for j in range(3):
        slot = jnp.where(row < 6, row, jnp.where(row == 6, j, 3 + j))
        picks.append(jnp.where(before == slot.astype(F32), named, 0.0))
    return picks, weight, row


def pack_matrix(j):
    q = iota((192, 256), 1)
    r = iota((192, 256), 0)
    s = q & 7
    base = (q >> 3) * 6
    if j < 0:
        return ((s < 6) & (r == base + s)).astype(F32).astype(BF16)
    return ((s >= 6) & (r == base + (s - 6) * 3 + j)).astype(F32).astype(BF16)


def fold_matrix(j):
    q = iota((256, 192), 0)
    r = iota((256, 192), 1)
    s = q & 7
    base = (q >> 3) * 6
    if j < 0:
        return ((s < 6) & (r == base + s)).astype(F32).astype(BF16)
    return ((s >= 6) & (r == base + (s - 6) * 3 + j)).astype(F32).astype(BF16)


ORDERS = ((2, 0, 1), (0, 1, 2), (1, 2, 0))
CHUNK = 512
CHUNKS = 8
SCALE = 1.0 / math.sqrt(NOPE + ROPE)


def layer_kernel(
    offs, rt_h, gt_h, hid_h, cot_h, lat_h, rope_h, qn_h, qp_h, wuv_h, wuk_h, wout_h, wg, wu, wd,
    own_h, dq_h, dp_h, out,
    rt, gt, hid, cot, rope, qn, qp, wout, own_out, dq_out, dp_out,
    send, recv, wgb, wub, wdb, back, landed, keys, gathered, comb, xs, dys, sc,
    wkv, qc, gx, dd, terms, r0, r1, ry, a1, r2, a2, r3,
    fsem, osem, sync, lsem, psem, ssem, rsem, wssem, wrsem, bssem, brsem, asem, bsem, gsem, hsem,
    s0, t0, s1, t1, sy, ty, ss, rs,
):
    y, x, z, c = place()
    coord = (y, x, z)
    me = (y * 4 + x) * 4 + z
    partner = (y * 4 + x, z * 2 + 1 - c)

    def peer(k, sign=1):
        k = (k * 11) % 64
        pw = ((y + 4 + sign * (k // 16)) % 4) * 4 + (x + 4 + sign * ((k // 4) % 4)) % 4
        pz = (z + 4 + sign * (k % 4)) % 4
        return pw * 4 + pz, (pw, pz * 2 + c)

    def device(d, o):
        at = list(coord)
        at[d] = (at[d] + o) % 4
        return (at[0] * 4 + at[1], at[2] * 2 + c)

    def remote(src, dst, a, b, dev):
        return pltpu.make_async_remote_copy(
            src_ref=src, dst_ref=dst, send_sem=a, recv_sem=b, device_id=dev, device_id_type=MESH
        )

    bar = pltpu.get_barrier_semaphore()

    pl.semaphore_signal(bar, inc=1, device_id=partner, device_id_type=MESH)
    for d in range(3):
        for o in range(1, 4):
            pl.semaphore_signal(bar, inc=1, device_id=device(d, o), device_id_type=MESH)
    fetches = [
        (rt_h, rt), (gt_h, gt), (hid_h, hid), (cot_h, cot), (rope_h, rope),
        (lat_h.at[pl.ds(128 * c, 64)], keys.at[y, x, c, 0, :, pl.ds(0, 512)]),
        (lat_h.at[pl.ds(128 * c + 64, 64)], keys.at[y, x, c, 1, :, pl.ds(0, 512)]),
        (qn_h, qn), (qp_h, qp), (wuv_h, wkv.at[pl.ds(0, 256)]), (wuk_h, wkv.at[pl.ds(256, 256)]),
        (wout_h, wout),
    ]
    fetches = [pltpu.make_async_copy(a, b, fsem.at[i]) for i, (a, b) in enumerate(fetches)]
    for q in fetches:
        q.start()
    weights = ((wg, wgb), (wu, wub), (wd, wdb))
    loads = [pltpu.make_async_copy(a, b.at[0], lsem.at[i]) for i, (a, b) in enumerate(weights)]
    for q in loads:
        q.start()
    for q in fetches[:7]:
        q.wait()
    eye = (iota((64, 128), 0) == iota((64, 128), 1)).astype(F32).astype(BF16)
    turned = dot(rope[...], eye, TN).astype(BF16).reshape(2, 2, 64, 128)
    for h in range(2):

        @pl.when(c == h)
        def _(h=h):
            keys[y, x, h, :, :, 512:640] = turned[h]

    pl.semaphore_wait(bar, 10)
    spread = []
    for k, d in ((0, 1), (1, 0)):
        for o in range(1, 4):
            at = keys.at[y, x, c, k]
            spread.append(remote(at, at, asem.at[0, k, o - 1], bsem.at[0, k, o - 1], device(d, o)))
    for q in spread:
        q.start()
    for o in range(1, 4):
        pl.semaphore_signal(sync.at[0], inc=1, device_id=device(0, o), device_id_type=MESH)

    picks, weight, row = selections(rt[...], gt[...])
    cot_hi = cot[:, 1024:2048]
    for j in range(3):
        if j == 1:
            pl.semaphore_wait(sync.at[0], 3)
            for o in range(1, 4):
                pl.semaphore_signal(sync.at[1], inc=1, device_id=device(2, o), device_id_type=MESH)
        low = jnp.where(row < 6, picks[j], 0.0).astype(BF16)
        high = jnp.where(row < 6, 0.0, picks[j]).astype(BF16)
        if j == 0:
            comb[0] = low
        comb[1 + j] = high
        part = (hid[:, 0:1024], hid[:, 1024:2048], cot[:, 0:1024])[j]
        gate = jnp.sum(picks[j] * weight, axis=1, keepdims=True)
        if j < 2:
            gate = jnp.where(row[:, 0:1] < 6, 1.0, gate)
        val = (dot(low, part) + dot(high, cot_hi)) * gate
        send[:, :, 1024 * j : 1024 * (j + 1)] = val.astype(BF16).reshape(64, 8, 1024)
    zero = jnp.zeros((256, 64), BF16)
    pl.semaphore_wait(sync.at[1], 3)

    def start(k, _):
        pc, dev = peer(k)
        remote(send.at[pc], recv.at[k], ssem.at[k], rsem.at[k], dev).start()
        return 0

    trades = [
        remote(a, b.at[1], wssem.at[i], wrsem.at[i], partner) for i, (a, b) in enumerate(weights)
    ]
    own = pltpu.make_async_copy(send.at[me], recv.at[0], psem)
    own.start()
    lax.fori_loop(1, 64, start, 0)
    for q in trades:
        q.start()
    for q in fetches[7:]:
        q.wait()
    for h in range(2):
        qc[h, :, 0:128] = qn[:, 128 * h : 128 * (h + 1)]
        qc[h, :, 128:256] = jnp.concatenate([qp[:, 64 * h : 64 * (h + 1)], zero], axis=1)
    own.wait()

    def arrive(k, _):
        remote(send.at[0], recv.at[k], ssem.at[k], rsem.at[k], partner).wait_recv()
        return 0

    def ret_start(k, _):
        remote(back.at[k], landed.at[me], bssem.at[k], brsem.at[me], peer(k, -1)[1]).start()
        return 0

    widen = []
    for k, d in ((0, 0), (1, 1)):
        for o in range(1, 4):
            at = keys.at[y, :, c, 0] if k == 0 else keys.at[:, x, c, 1]
            widen.append(remote(at, at, asem.at[1, k, o - 1], bsem.at[1, k, o - 1], device(d, o)))
    mirror = remote(keys.at[:, :, c], keys.at[:, :, c], gsem.at[4], hsem.at[4], partner)

    for g in range(2):
        lax.fori_loop(max(1, 32 * g), 32 * (g + 1), arrive, 0)
        plain = pack_matrix(-1)

        def cols(a, b, g=g):
            return recv[32 * g : 32 * (g + 1), :, a:b].reshape(256, b - a)

        xs[:, 0:1024] = dot(plain, cols(0, 1024)).astype(BF16)
        xs[:, 1024:2048] = dot(plain, cols(1024, 2048)).astype(BF16)
        dys[:, 0:1024] = dot(plain, cols(2048, 3072)).astype(BF16)
        hi = dot(pack_matrix(0), cols(0, 1024))
        hi = hi + dot(pack_matrix(1), cols(1024, 2048))
        hi = hi + dot(pack_matrix(2), cols(2048, 3072))
        dys[:, 1024:2048] = hi.astype(BF16)
        if g == 0:
            for q in loads:
                q.wait()
        for h in range(2):
            if g == 0 and h == 1:
                for q in trades:
                    q.wait()
            if g == 1 and h == 1:
                for q in widen:
                    q.wait()
                mirror.start()
            pre = dot(xs[...], wgb[h], NT)
            up = dot(xs[...], wub[h], NT)
            gh = dot(dys[...], wdb[h], NT)
            s = jax.nn.sigmoid(pre)
            gg = (gh * up * s * (1.0 + pre * (1.0 - s))).astype(BF16)
            gu = (gh * pre * s).astype(BF16)
            for b in range(2):
                cs = slice(1024 * b, 1024 * (b + 1))
                term = dot(gg, wgb[h, :, cs]) + dot(gu, wub[h, :, cs])
                if h == 0:
                    sc[0, 0:192, cs] = term
                else:
                    xs[:, cs] = (sc[0, 0:192, cs] + term).astype(BF16)
        plain = fold_matrix(-1)
        for j in range(3):
            val = dot(plain, xs[:, 512 * j : 512 * (j + 1)])
            val = val + dot(fold_matrix(j), xs[:, 1536:2048])
            back[32 * g : 32 * (g + 1), :, 512 * j : 512 * (j + 1)] = val.astype(BF16).reshape(32, 8, 512)
        if g == 0:
            for q in spread:
                q.wait()
            for q in widen:
                q.start()
            own = pltpu.make_async_copy(back.at[0], landed.at[me], psem)
            own.start()
        lax.fori_loop(max(1, 32 * g), 32 * (g + 1), ret_start, 0)

    mirror.wait()
    ones = (iota((CHUNK, 128), 1) < 2).astype(F32).astype(BF16)
    delta = iota((256, 256), 0) - iota((256, 256), 1)
    here = offs[y * 4 + x]

    def block(i):
        return slice(0, CHUNK), pl.ds(pl.multiple_of(i * 256, 256), 256)

    def forward(i, tops):
        sub, at = block(i)
        chunk = keys[i // 2, pl.ds((i % 2) * 2, 2)].reshape(CHUNK, 640)
        kv = dot(chunk[:, 0:512], wkv[...], NT).astype(BF16)
        new = []
        for h in range(2):
            vx = jnp.concatenate([kv[:, 128 * h : 128 * (h + 1)], ones], axis=1)
            kc = jnp.concatenate([kv[:, 256 + 128 * h : 256 + 128 * (h + 1)], chunk[:, 512:640]], axis=1)
            wdb[h, sub, at] = vx
            wub[h, sub, at] = kc
            top = tops[h]
            val = dot(kc, qc[h], NT)
            for b in range(2):
                limit = (here - offs[2 * i + b]) * 256
                part = jnp.where(delta <= limit, val[256 * b : 256 * (b + 1)], -1e30)
                sc[h, 256 * b : 256 * (b + 1), at] = part
                top = jnp.maximum(top, jnp.max(part.reshape(32, 8, 256), axis=0))
            new.append(top)
        return tuple(new)

    least = jnp.full((8, 256), -1e30, F32)
    tops = lax.fori_loop(0, CHUNKS, forward, (least, least))
    tops = [jnp.max(t, axis=0, keepdims=True) for t in tops]

    def weigh(i, sums):
        sub, at = block(i)
        new = []
        for h in range(2):
            p = jnp.exp(SCALE * (sc[h, sub, at] - tops[h])).astype(BF16)
            wgb[h, sub, at] = p
            new.append(sums[h] + dot(p, wdb[h, sub, at], TN))
        return tuple(new)

    nil = jnp.zeros((256, 256), F32)
    sums = lax.fori_loop(0, CHUNKS, weigh, (nil, nil))

    own.wait()

    def ret_finish(k, _):
        pc = peer(k)[0]
        remote(send.at[0], recv.at[k], ssem.at[k], rsem.at[k], partner).wait_send()
        q = remote(back.at[k], landed.at[pc], bssem.at[k], brsem.at[pc], partner)
        q.wait_send()
        q.wait_recv()
        return 0

    lax.fori_loop(1, 64, ret_finish, 0)

    total = cot[...].astype(F32)
    rest = jnp.zeros((32, 512), F32)
    for j in range(3):
        part = landed[:, :, 512 * j : 512 * (j + 1)].reshape(512, 512)
        cs = slice(512 * j, 512 * (j + 1))
        own_out[:, cs] = (total[:, cs] + dot(comb[0], part, TN)).astype(BF16)
        rest = rest + dot(comb[1 + j], part, TN)
    own_out[:, 1536:2048] = (total[:, 1536:2048] + rest).astype(BF16)
    gathered[z, c] = own_out[...]
    writes = [
        pltpu.make_async_copy(a, b, osem.at[i])
        for i, (a, b) in enumerate(((own_out, own_h), (dq_out, dq_h), (dp_out, dp_h)))
    ]
    writes[0].start()
    hops = [
        remote(own_out, gathered.at[z, c], gsem.at[o - 1], hsem.at[o - 1], device(2, o))
        for o in range(1, 4)
    ]
    for q in hops:
        q.start()
    for q in hops:
        q.wait()
    last = remote(gathered.at[:, c], gathered.at[:, c], gsem.at[3], hsem.at[3], partner)
    last.start()
    last.wait()

    go = dot(gathered[...].reshape(256, 2048), wout[...], NT).astype(BF16).astype(F32)
    lane = iota((256, 128), 1)
    for h in range(2):
        inv = 1.0 / sums[h][:, 128:129]
        mean = sums[h][:, 0:128] * inv
        scaled = (go[:, 128 * h : 128 * (h + 1)] * inv).astype(BF16)
        drop = -jnp.sum(scaled.astype(F32) * mean, axis=1, keepdims=True)
        high = drop.astype(BF16).astype(F32)
        extra = jnp.where(lane == 0, high, jnp.where(lane == 1, drop - high, 0.0))
        gx[h, :, 0:128] = scaled
        gx[h, :, 128:256] = extra.astype(BF16)

    def trade(r):
        g = (y + 1 + r) % 4
        return remote(terms.at[1 - c, g], r0.at[g], s0.at[r], t0.at[r], partner)

    left = iota((16, 128), 1) < 64

    def backward(i, dqs):
        sub, at = block(i)
        new = []
        ropes = 0.0
        for h in range(2):
            p = wgb[h, sub, at]
            diff = dot(wdb[h, sub, at], gx[h], NT)
            ds = (p.astype(F32) * diff).astype(BF16)
            new.append(dqs[h] + dot(ds, wub[h, sub, at], TN))
            dk = dot(ds, qc[h]) * SCALE
            dd[:, 128 * h : 128 * (h + 1)] = dot(p, gx[h, :, 0:128]).astype(BF16)
            dd[:, 256 + 128 * h : 256 + 128 * (h + 1)] = dk[:, 0:128].astype(BF16)
            ropes = ropes + dk[:, 128:256]
        turned = pltpu.roll(ropes, 64, 1)
        tl = dot(dd[...], wkv[...]).astype(BF16)
        for q in range(16):
            e, f, m = i // 2, (i % 2) * 2 + q // 8, (q // 2) % 4
            for l in range(4):
                terms[q % 2, e, f, m, 32 * l : 32 * (l + 1), :] = tl[32 * q : 32 * (q + 1), 128 * l : 128 * (l + 1)]
            terms[q % 2, e, f, m, 128:144, :] = jnp.where(
                left, ropes[32 * q : 32 * q + 16], turned[32 * q + 16 : 32 * q + 32]
            ).astype(BF16)
        return tuple(new)

    def near(r, k, o):
        g = (y + 1 + r) % 4
        d = ORDERS[k][0]
        rows = pl.ds(48 * k, 48)
        to = (coord[d] + o) % 4
        src = terms.at[c, g, :, to, rows] if k == 0 else terms.at[c, g, to, :, rows]
        i = k // 2
        return remote(src, r1.at[i, o - 1, g], s1.at[i, o - 1, r], t1.at[i, o - 1, r], device(d, o))

    def far(r):
        g = (y + 1 + r) % 4
        pz = z * 2 + c
        return remote(terms.at[c, g, :, :, pl.ds(48, 48)], ry.at[r], sy.at[r], ty.at[r], (g * 4 + x, pz))

    def settle(r):
        trade(r).wait()
        g = (y + 1 + r) % 4

        def add(i, _):
            a, b = i // 4, i % 4
            val = terms[c, g, a, b].astype(F32) + r0[g, a, b].astype(F32)
            terms[c, g, a, b] = val.astype(BF16)
            return 0

        lax.fori_loop(0, 16, add, 0)
        for o in range(1, 4):
            near(r, 0, o).start()
            near(r, 2, o).start()

        @pl.when(r < 3)
        def _():
            far(r).start()

    def quarter(r, dqs):
        i = ((y + 1 + r) % 4) * 2
        dqs = lax.fori_loop(i, i + 2, backward, dqs)
        trade(r).start()

        @pl.when(r > 0)
        def _():
            settle(r - 1)

        return dqs

    dqs = lax.fori_loop(0, 4, quarter, (nil, nil))
    for h in range(2):
        val = (dqs[h] * SCALE).astype(BF16)
        dq_out[:, 128 * h : 128 * (h + 1)] = val[:, 0:128]
        dp_out[:, 64 * h : 64 * (h + 1)] = val[:, 128:192]
    writes[1].start()
    writes[2].start()
    settle(3)

    def close(r, _):
        for o in range(1, 4):
            near(r, 0, o).wait()
            near(r, 2, o).wait()

        @pl.when(r < 3)
        def _():
            far(r).wait()

        return 0

    lax.fori_loop(0, 4, close, 0)

    def add1(i, _):
        a, b = i // 4, i % 4
        val = terms[c, a, b, z, 0:48].astype(F32)
        for o in range(3):
            val = val + r1[0, o, a, b].astype(F32)
        a1[0, a, b] = val.astype(BF16)
        val = terms[c, y, a, b, 48:96].astype(F32)
        for o in range(3):
            val = val + ry[o, a, b].astype(F32)
        a1[1, a, b] = val.astype(BF16)
        val = terms[c, a, x, b, 96:144].astype(F32)
        for o in range(3):
            val = val + r1[1, o, a, b].astype(F32)
        a1[2, b, a] = val.astype(BF16)
        return 0

    lax.fori_loop(0, 16, add1, 0)

    def stage(i, src, dst):
        copies = []
        for o in range(1, 4):
            for k in range(3):
                d = ORDERS[k][i]
                copies.append(
                    remote(
                        src.at[k, (coord[d] + o) % 4], dst.at[k, o - 1],
                        ss.at[i - 1, k, o - 1], rs.at[i - 1, k, o - 1], device(d, o),
                    )
                )
        for q in copies:
            q.start()
        for q in copies:
            q.wait()

    stage(1, a1, r2)
    for k in range(3):
        val = a1[k, coord[ORDERS[k][1]]].astype(F32)
        for o in range(3):
            val = val + r2[k, o].astype(F32)
        a2[k] = val.astype(BF16)
    stage(2, a2, r3)
    for k in range(3):
        val = a2[k, coord[ORDERS[k][2]]].astype(F32)
        for o in range(3):
            val = val + r3[k, o].astype(F32)
        out[48 * k : 48 * (k + 1), :] = val
    for q in writes:
        q.wait()


def layer(*args):
    vm = pl.BlockSpec(memory_space=pltpu.VMEM)
    sm = pl.BlockSpec(memory_space=pltpu.SMEM)
    hbm = pl.BlockSpec(memory_space=pl.ANY)
    dma = pltpu.SemaphoreType.DMA
    half = args[-1].shape[0]

    def room(*shape, dtype=BF16):
        return pltpu.VMEM(shape, dtype)

    return pl.pallas_call(
        layer_kernel,
        out_shape=(
            jax.ShapeDtypeStruct((32, 2048), BF16),
            jax.ShapeDtypeStruct((256, 256), BF16),
            jax.ShapeDtypeStruct((256, 128), BF16),
            jax.ShapeDtypeStruct((144, 128), F32),
        ),
        in_specs=[sm] + [hbm] * 14,
        out_specs=(hbm, hbm, hbm, vm),
        scratch_shapes=[
            room(6, 32, dtype=jnp.int32), room(6, 32, dtype=F32), room(32, 2048), room(32, 2048),
            room(64, 256), room(256, 256), room(256, 128), room(256, 2048),
            room(32, 2048), room(256, 256), room(256, 128),
            room(64, 8, 3072), room(64, 8, 3072),
            room(2, half, 2048), room(2, half, 2048), room(2, half, 2048),
            room(64, 8, 1536), room(64, 8, 1536),
            room(4, 4, 2, 2, 64, 640), room(4, 2, 32, 2048), room(4, 512, 32),
            room(192, 2048), room(192, 2048), room(2, 512, 2048, dtype=F32),
            room(512, 512), room(2, 256, 256), room(2, 256, 256), room(CHUNK, 512),
            room(2, 4, 4, 4, 144, 128), room(4, 4, 4, 144, 128),
            room(2, 3, 4, 4, 48, 128), room(3, 4, 4, 48, 128),
            room(3, 4, 4, 48, 128), room(3, 3, 4, 48, 128),
            room(3, 4, 48, 128), room(3, 3, 48, 128),
            dma((12,)), dma((3,)), pltpu.SemaphoreType.REGULAR((2,)),
            dma((3,)), dma, dma((64,)), dma((64,)), dma((3,)), dma((3,)),
            dma((64,)), dma((64,)), dma((2, 2, 3)), dma((2, 2, 3)), dma((5,)), dma((5,)),
            dma((4,)), dma((4,)), dma((2, 3, 4)), dma((2, 3, 4)), dma((3,)), dma((3,)),
            dma((2, 3, 3)), dma((2, 3, 3)),
        ],
        compiler_params=pltpu.CompilerParams(
            collective_id=0, has_side_effects=True, vmem_limit_bytes=67043328
        ),
        cost_estimate=pl.CostEstimate(flops=22 * 10**9, bytes_accessed=20 * 10**6, transcendentals=3 * 10**6),
    )(*args)


def lay_kernel(own, dq, dp, sums, own_out, dq_out, dp_out, lat_out, rope_out):
    own_out[...] = own[...]
    dq_out[...] = dq[...]
    dp_out[...] = dp[...]
    for l in range(4):
        lat_out[:, 128 * l : 128 * (l + 1)] = sums[32 * l : 32 * (l + 1), :]
    rope_out[0:16, :] = sums[128:144, 0:64]
    rope_out[16:32, :] = sums[128:144, 64:128]


def lay_out(*args):
    vm = pl.BlockSpec(memory_space=pltpu.VMEM)
    return pl.pallas_call(
        lay_kernel,
        out_shape=(
            jax.ShapeDtypeStruct((32, 2048), BF16),
            jax.ShapeDtypeStruct((256, 256), BF16),
            jax.ShapeDtypeStruct((256, 128), BF16),
            jax.ShapeDtypeStruct((32, 512), F32),
            jax.ShapeDtypeStruct((32, 64), F32),
        ),
        in_specs=[vm] * 4,
        out_specs=(vm,) * 5,
    )(*args)


def on_device(
    hidden, cotangent, routes, gates, offsets, w_gate, w_up, w_down, w_out,
    latent, rope_key, q_nope, q_pe, w_uk, w_uv,
):
    return lay_out(
        *layer(
            offsets, routes.T, gates.T, hidden, cotangent, latent, rope_key.T, q_nope, q_pe,
            w_uv, w_uk, w_out, w_gate[0].T, w_up[0].T, w_down[0],
        )
    )


def solution(mesh):
    both = ("wide", "narrow")
    return jax.shard_map(
        on_device,
        mesh=mesh,
        in_specs=(
            P(both, None), P(both, None), P(both, None), P(both, None), P(),
            P(both, None, None), P(both, None, None), P(both, None, None),
            P("narrow", None), P("wide", None), P("wide", None),
            P("wide", "narrow"), P("wide", "narrow"), P("narrow", None), P("narrow", None),
        ),
        out_specs=(
            P(both, None), P("wide", "narrow"), P("wide", "narrow"), P(both, None), P(both, None),
        ),
        check_vma=False,
    )
```

```python
import functools
import math

import jax
import jax.numpy as jnp
from jax import lax
from jax.experimental import pallas as pl
from jax.experimental.pallas import tpu as pltpu
from jax.sharding import PartitionSpec as P

LATENT = 512
NOPE = 128
ROPE = 64
VDIM = 128
MESH = pl.DeviceIdType.MESH
F32 = jnp.float32
BF16 = jnp.bfloat16
NT = (((1,), (1,)), ((), ()))
NN = (((1,), (0,)), ((), ()))
TN = (((0,), (0,)), ((), ()))


def dot(a, b, dims=NN):
    return lax.dot_general(a, b, dims, preferred_element_type=F32)


def iota(shape, dim):
    return lax.broadcasted_iota(jnp.int32, shape, dim)


def place():
    w = lax.axis_index("wide")
    n = lax.axis_index("narrow")
    return w // 4, w % 4, n // 2, n % 2


def selections(rt, gt):
    expert = iota((512, 32), 0) >> 3
    named = jnp.zeros((512, 32), F32)
    weight = jnp.zeros((512, 32), F32)
    for k in range(6):
        hit = expert == rt[k : k + 1, :]
        named = jnp.where(hit, 1.0, named)
        weight = jnp.where(hit, gt[k : k + 1, :], weight)
    earlier = (iota((32, 32), 0) < iota((32, 32), 1)).astype(F32).astype(BF16)
    before = dot(named.astype(BF16), earlier)
    row = iota((512, 32), 0) & 7
    picks = []
    for j in range(3):
        slot = jnp.where(row < 6, row, jnp.where(row == 6, j, 3 + j))
        picks.append(jnp.where(before == slot.astype(F32), named, 0.0))
    return picks, weight, row


def pack_matrix(j):
    q = iota((192, 256), 1)
    r = iota((192, 256), 0)
    s = q & 7
    base = (q >> 3) * 6
    if j < 0:
        return ((s < 6) & (r == base + s)).astype(F32).astype(BF16)
    return ((s >= 6) & (r == base + (s - 6) * 3 + j)).astype(F32).astype(BF16)


def fold_matrix(j):
    q = iota((256, 192), 0)
    r = iota((256, 192), 1)
    s = q & 7
    base = (q >> 3) * 6
    if j < 0:
        return ((s < 6) & (r == base + s)).astype(F32).astype(BF16)
    return ((s >= 6) & (r == base + (s - 6) * 3 + j)).astype(F32).astype(BF16)


ORDERS = ((2, 0, 1), (0, 1, 2), (1, 2, 0))
CHUNK = 512
CHUNKS = 8
SCALE = 1.0 / math.sqrt(NOPE + ROPE)


def layer_kernel(
    offs, rt_h, gt_h, hid_h, cot_h, lat_h, rope_h, qn_h, qp_h, wuv_h, wuk_h, wout_h, wg, wu, wd,
    own_h, dq_h, dp_h, out,
    rt, gt, hid, cot, rope, qn, qp, wout, own_out, dq_out, dp_out,
    send, recv, wgb, wub, wdb, back, landed, keys, gathered, comb, xs, dys, sc,
    wkv, qc, gx, dd, terms, r0, r1, ry, a1, r2, a2, r3,
    fsem, osem, sync, lsem, psem, ssem, rsem, wssem, wrsem, bssem, brsem, asem, bsem, gsem, hsem, psem2, qsem2,
    s0, t0, s1, t1, sy, ty, ss, rs,
):
    y, x, z, c = place()
    coord = (y, x, z)
    me = (y * 4 + x) * 4 + z
    partner = (y * 4 + x, z * 2 + 1 - c)

    def peer(k, sign=1):
        k = (k * 11) % 64
        pw = ((y + 4 + sign * (k // 16)) % 4) * 4 + (x + 4 + sign * ((k // 4) % 4)) % 4
        pz = (z + 4 + sign * (k % 4)) % 4
        return pw * 4 + pz, (pw, pz * 2 + c)

    def device(d, o):
        at = list(coord)
        at[d] = (at[d] + o) % 4
        return (at[0] * 4 + at[1], at[2] * 2 + c)

    def remote(src, dst, a, b, dev):
        return pltpu.make_async_remote_copy(
            src_ref=src, dst_ref=dst, send_sem=a, recv_sem=b, device_id=dev, device_id_type=MESH
        )

    bar = pltpu.get_barrier_semaphore()

    pl.semaphore_signal(bar, inc=1, device_id=partner, device_id_type=MESH)
    for d in range(3):
        for o in range(1, 4):
            pl.semaphore_signal(bar, inc=1, device_id=device(d, o), device_id_type=MESH)
    fetches = [
        (rt_h, rt), (gt_h, gt), (hid_h, hid), (cot_h, cot), (rope_h, rope),
        (lat_h.at[pl.ds(128 * c, 64)], keys.at[y, x, c, 0, :, pl.ds(0, 512)]),
        (lat_h.at[pl.ds(128 * c + 64, 64)], keys.at[y, x, c, 1, :, pl.ds(0, 512)]),
        (qn_h, qn), (qp_h, qp), (wuv_h, wkv.at[pl.ds(0, 256)]), (wuk_h, wkv.at[pl.ds(256, 256)]),
        (wout_h, wout),
    ]
    fetches = [pltpu.make_async_copy(a, b, fsem.at[i]) for i, (a, b) in enumerate(fetches)]
    for q in fetches:
        q.start()
    weights = ((wg, wgb), (wu, wub), (wd, wdb))
    loads = [pltpu.make_async_copy(a, b.at[0], lsem.at[i]) for i, (a, b) in enumerate(weights)]
    for q in loads:
        q.start()
    for q in fetches[:7]:
        q.wait()
    eye = (iota((64, 128), 0) == iota((64, 128), 1)).astype(F32).astype(BF16)
    turned = dot(rope[...], eye, TN).astype(BF16).reshape(2, 2, 64, 128)
    for h in range(2):

        @pl.when(c == h)
        def _(h=h):
            keys[y, x, h, :, :, 512:640] = turned[h]

    pl.semaphore_wait(bar, 10)
    spread = []
    for k, d in ((0, 1), (1, 0)):
        for o in range(1, 4):
            at = keys.at[y, x, c, k]
            spread.append(remote(at, at, asem.at[0, k, o - 1], bsem.at[0, k, o - 1], device(d, o)))
    for q in spread:
        q.start()
    for o in range(1, 4):
        pl.semaphore_signal(sync.at[0], inc=1, device_id=device(0, o), device_id_type=MESH)

    picks, weight, row = selections(rt[...], gt[...])
    cot_hi = cot[:, 1024:2048]
    for j in range(3):
        if j == 1:
            pl.semaphore_wait(sync.at[0], 3)
            for o in range(1, 4):
                pl.semaphore_signal(sync.at[1], inc=1, device_id=device(2, o), device_id_type=MESH)
        low = jnp.where(row < 6, picks[j], 0.0).astype(BF16)
        high = jnp.where(row < 6, 0.0, picks[j]).astype(BF16)
        if j == 0:
            comb[0] = low
        comb[1 + j] = high
        part = (hid[:, 0:1024], hid[:, 1024:2048], cot[:, 0:1024])[j]
        gate = jnp.sum(picks[j] * weight, axis=1, keepdims=True)
        if j < 2:
            gate = jnp.where(row[:, 0:1] < 6, 1.0, gate)
        val = (dot(low, part) + dot(high, cot_hi)) * gate
        send[:, :, 1024 * j : 1024 * (j + 1)] = val.astype(BF16).reshape(64, 8, 1024)
    zero = jnp.zeros((256, 64), BF16)
    pl.semaphore_wait(sync.at[1], 3)

    def start(k, _):
        pc, dev = peer(k)
        remote(send.at[pc], recv.at[k], ssem.at[k], rsem.at[k], dev).start()
        return 0

    trades = [
        remote(a, b.at[1], wssem.at[i], wrsem.at[i], partner) for i, (a, b) in enumerate(weights)
    ]
    own = pltpu.make_async_copy(send.at[me], recv.at[0], psem)
    own.start()
    lax.fori_loop(1, 64, start, 0)
    for q in trades:
        q.start()
    for q in fetches[7:]:
        q.wait()
    for h in range(2):
        qc[h, :, 0:128] = qn[:, 128 * h : 128 * (h + 1)]
        qc[h, :, 128:256] = jnp.concatenate([qp[:, 64 * h : 64 * (h + 1)], zero], axis=1)
    own.wait()

    def arrive(k, _):
        remote(send.at[0], recv.at[k], ssem.at[k], rsem.at[k], partner).wait_recv()
        return 0

    def ret_start(k, _):
        remote(back.at[k], landed.at[me], bssem.at[k], brsem.at[me], peer(k, -1)[1]).start()
        return 0

    widen = []
    for k, d in ((0, 0), (1, 1)):
        for o in range(1, 4):
            at = keys.at[y, :, c, 0] if k == 0 else keys.at[:, x, c, 1]
            widen.append(remote(at, at, asem.at[1, k, o - 1], bsem.at[1, k, o - 1], device(d, o)))
    mirror = remote(keys.at[:, :, c], keys.at[:, :, c], gsem.at[4], hsem.at[4], partner)

    for g in range(2):
        lax.fori_loop(max(1, 32 * g), 32 * (g + 1), arrive, 0)
        plain = pack_matrix(-1)

        def cols(a, b, g=g):
            return recv[32 * g : 32 * (g + 1), :, a:b].reshape(256, b - a)

        xs[:, 0:1024] = dot(plain, cols(0, 1024)).astype(BF16)
        xs[:, 1024:2048] = dot(plain, cols(1024, 2048)).astype(BF16)
        dys[:, 0:1024] = dot(plain, cols(2048, 3072)).astype(BF16)
        hi = dot(pack_matrix(0), cols(0, 1024))
        hi = hi + dot(pack_matrix(1), cols(1024, 2048))
        hi = hi + dot(pack_matrix(2), cols(2048, 3072))
        dys[:, 1024:2048] = hi.astype(BF16)
        if g == 0:
            for q in loads:
                q.wait()
        for h in range(2):
            if g == 0 and h == 1:
                for q in trades:
                    q.wait()
            if g == 1 and h == 1:
                for q in widen:
                    q.wait()
                mirror.start()
            pre = dot(xs[...], wgb[h], NT)
            up = dot(xs[...], wub[h], NT)
            gh = dot(dys[...], wdb[h], NT)
            s = jax.nn.sigmoid(pre)
            gg = (gh * up * s * (1.0 + pre * (1.0 - s))).astype(BF16)
            gu = (gh * pre * s).astype(BF16)
            for b in range(2):
                cs = slice(1024 * b, 1024 * (b + 1))
                term = dot(gg, wgb[h, :, cs]) + dot(gu, wub[h, :, cs])
                if h == 0:
                    sc[0, 0:192, cs] = term
                else:
                    xs[:, cs] = (sc[0, 0:192, cs] + term).astype(BF16)
        plain = fold_matrix(-1)
        for j in range(3):
            val = dot(plain, xs[:, 512 * j : 512 * (j + 1)])
            val = val + dot(fold_matrix(j), xs[:, 1536:2048])
            back[32 * g : 32 * (g + 1), :, 512 * j : 512 * (j + 1)] = val.astype(BF16).reshape(32, 8, 512)
        if g == 0:
            for q in spread:
                q.wait()
            for q in widen:
                q.start()
            own = pltpu.make_async_copy(back.at[0], landed.at[me], psem)
            own.start()
        lax.fori_loop(max(1, 32 * g), 32 * (g + 1), ret_start, 0)

    mirror.wait()
    ones = (iota((CHUNK, 128), 1) < 2).astype(F32).astype(BF16)
    delta = iota((256, 256), 0) - iota((256, 256), 1)
    here = offs[y * 4 + x]

    def block(i):
        return slice(0, CHUNK), pl.ds(pl.multiple_of(i * 256, 256), 256)

    def forward(i, tops):
        sub, at = block(i)
        chunk = keys[i // 2, pl.ds((i % 2) * 2, 2)].reshape(CHUNK, 640)
        kv = dot(chunk[:, 0:512], wkv[...], NT).astype(BF16)
        new = []
        for h in range(2):
            vx = jnp.concatenate([kv[:, 128 * h : 128 * (h + 1)], ones], axis=1)
            kc = jnp.concatenate([kv[:, 256 + 128 * h : 256 + 128 * (h + 1)], chunk[:, 512:640]], axis=1)
            wdb[h, sub, at] = vx
            wub[h, sub, at] = kc
            top = tops[h]
            val = dot(kc, qc[h], NT)
            for b in range(2):
                limit = (here - offs[2 * i + b]) * 256
                part = jnp.where(delta <= limit, val[256 * b : 256 * (b + 1)], -1e30)
                sc[h, 256 * b : 256 * (b + 1), at] = part
                top = jnp.maximum(top, jnp.max(part.reshape(32, 8, 256), axis=0))
            new.append(top)
        return tuple(new)

    least = jnp.full((8, 256), -1e30, F32)
    tops = lax.fori_loop(0, CHUNKS, forward, (least, least))
    tops = [jnp.max(t, axis=0, keepdims=True) for t in tops]

    def weigh(i, sums):
        sub, at = block(i)
        new = []
        for h in range(2):
            p = jnp.exp(SCALE * (sc[h, sub, at] - tops[h])).astype(BF16)
            wgb[h, sub, at] = p
            new.append(sums[h] + dot(p, wdb[h, sub, at], TN))
        return tuple(new)

    nil = jnp.zeros((256, 256), F32)
    sums = lax.fori_loop(0, CHUNKS, weigh, (nil, nil))

    own.wait()

    def ret_finish(k, _):
        pc = peer(k)[0]
        remote(back.at[k], landed.at[pc], bssem.at[k], brsem.at[pc], partner).wait_recv()
        return 0

    def sent(k, _):
        remote(send.at[0], recv.at[k], ssem.at[k], rsem.at[k], partner).wait_send()
        remote(back.at[k], landed.at[me], bssem.at[k], brsem.at[me], partner).wait_send()
        return 0

    lax.fori_loop(1, 64, ret_finish, 0)

    total = cot[...].astype(F32)
    rest = jnp.zeros((32, 512), F32)
    for j in range(3):
        part = landed[:, :, 512 * j : 512 * (j + 1)].reshape(512, 512)
        cs = slice(512 * j, 512 * (j + 1))
        own_out[:, cs] = (total[:, cs] + dot(comb[0], part, TN)).astype(BF16)
        rest = rest + dot(comb[1 + j], part, TN)
    own_out[:, 1536:2048] = (total[:, 1536:2048] + rest).astype(BF16)
    gathered[z, c] = own_out[...]
    writes = [
        pltpu.make_async_copy(a, b, osem.at[i])
        for i, (a, b) in enumerate(((own_out, own_h), (dq_out, dq_h), (dp_out, dp_h)))
    ]
    writes[0].start()
    hops = [
        remote(own_out, gathered.at[z, c], gsem.at[o - 1], hsem.at[o - 1], device(2, o))
        for o in range(1, 4)
    ]
    for q in hops:
        q.start()

    def pair(o):
        at = gathered.at[(z + 4 - o) % 4, c]
        return remote(at, at, psem2.at[o], qsem2.at[o], partner)

    pair(0).start()
    for o in range(1, 4):
        hops[o - 1].wait()
        pair(o).start()
    for o in range(4):
        pair(o).wait()

    go = dot(gathered[...].reshape(256, 2048), wout[...], NT).astype(BF16).astype(F32)
    lane = iota((256, 128), 1)
    for h in range(2):
        inv = 1.0 / sums[h][:, 128:129]
        mean = sums[h][:, 0:128] * inv
        scaled = (go[:, 128 * h : 128 * (h + 1)] * inv).astype(BF16)
        drop = -jnp.sum(scaled.astype(F32) * mean, axis=1, keepdims=True)
        high = drop.astype(BF16).astype(F32)
        extra = jnp.where(lane == 0, high, jnp.where(lane == 1, drop - high, 0.0))
        gx[h, :, 0:128] = scaled
        gx[h, :, 128:256] = extra.astype(BF16)

    def trade(r):
        g = (y + 1 + r) % 4
        return remote(terms.at[1 - c, g], r0.at[g], s0.at[r], t0.at[r], partner)

    left = iota((16, 128), 1) < 64

    def backward(i, dqs):
        sub, at = block(i)
        new = []
        ropes = 0.0
        for h in range(2):
            p = wgb[h, sub, at]
            diff = dot(wdb[h, sub, at], gx[h], NT)
            ds = (p.astype(F32) * diff).astype(BF16)
            new.append(dqs[h] + dot(ds, wub[h, sub, at], TN))
            dk = dot(ds, qc[h]) * SCALE
            dd[:, 128 * h : 128 * (h + 1)] = dot(p, gx[h, :, 0:128]).astype(BF16)
            dd[:, 256 + 128 * h : 256 + 128 * (h + 1)] = dk[:, 0:128].astype(BF16)
            ropes = ropes + dk[:, 128:256]
        turned = pltpu.roll(ropes, 64, 1)
        tl = dot(dd[...], wkv[...]).astype(BF16)
        for q in range(16):
            e, f, m = i // 2, (i % 2) * 2 + q // 8, (q // 2) % 4
            for l in range(4):
                terms[q % 2, e, f, m, 32 * l : 32 * (l + 1), :] = tl[32 * q : 32 * (q + 1), 128 * l : 128 * (l + 1)]
            terms[q % 2, e, f, m, 128:144, :] = jnp.where(
                left, ropes[32 * q : 32 * q + 16], turned[32 * q + 16 : 32 * q + 32]
            ).astype(BF16)
        return tuple(new)

    def near(r, k, o):
        g = (y + 1 + r) % 4
        d = ORDERS[k][0]
        rows = pl.ds(48 * k, 48)
        to = (coord[d] + o) % 4
        src = terms.at[c, g, :, to, rows] if k == 0 else terms.at[c, g, to, :, rows]
        i = k // 2
        return remote(src, r1.at[i, o - 1, g], s1.at[i, o - 1, r], t1.at[i, o - 1, r], device(d, o))

    def far(r):
        g = (y + 1 + r) % 4
        pz = z * 2 + c
        return remote(terms.at[c, g, :, :, pl.ds(48, 48)], ry.at[r], sy.at[r], ty.at[r], (g * 4 + x, pz))

    def settle(r):
        trade(r).wait()
        g = (y + 1 + r) % 4

        def add(i, _):
            a, b = i // 4, i % 4
            val = terms[c, g, a, b].astype(F32) + r0[g, a, b].astype(F32)
            terms[c, g, a, b] = val.astype(BF16)
            return 0

        lax.fori_loop(0, 16, add, 0)
        for o in range(1, 4):
            near(r, 0, o).start()
            near(r, 2, o).start()

        @pl.when(r < 3)
        def _():
            far(r).start()

    def quarter(r, dqs):
        i = ((y + 1 + r) % 4) * 2
        dqs = lax.fori_loop(i, i + 2, backward, dqs)
        trade(r).start()

        @pl.when(r > 0)
        def _():
            settle(r - 1)

        return dqs

    dqs = lax.fori_loop(0, 4, quarter, (nil, nil))
    for h in range(2):
        val = (dqs[h] * SCALE).astype(BF16)
        dq_out[:, 128 * h : 128 * (h + 1)] = val[:, 0:128]
        dp_out[:, 64 * h : 64 * (h + 1)] = val[:, 128:192]
    writes[1].start()
    writes[2].start()
    settle(3)

    def close(r, _):
        for o in range(1, 4):
            near(r, 0, o).wait()
            near(r, 2, o).wait()

        @pl.when(r < 3)
        def _():
            far(r).wait()

        return 0

    lax.fori_loop(0, 4, close, 0)

    def add1(i, _):
        a, b = i // 4, i % 4
        val = terms[c, a, b, z, 0:48].astype(F32)
        for o in range(3):
            val = val + r1[0, o, a, b].astype(F32)
        a1[0, a, b] = val.astype(BF16)
        val = terms[c, y, a, b, 48:96].astype(F32)
        for o in range(3):
            val = val + ry[o, a, b].astype(F32)
        a1[1, a, b] = val.astype(BF16)
        val = terms[c, a, x, b, 96:144].astype(F32)
        for o in range(3):
            val = val + r1[1, o, a, b].astype(F32)
        a1[2, b, a] = val.astype(BF16)
        return 0

    lax.fori_loop(0, 16, add1, 0)

    def stage(i, src, dst, beside=None):
        copies = []
        for o in range(1, 4):
            for k in range(3):
                d = ORDERS[k][i]
                copies.append(
                    remote(
                        src.at[k, (coord[d] + o) % 4], dst.at[k, o - 1],
                        ss.at[i - 1, k, o - 1], rs.at[i - 1, k, o - 1], device(d, o),
                    )
                )
        for q in copies:
            q.start()
        if beside:
            beside()
        for q in copies:
            q.wait()

    stage(1, a1, r2, lambda: lax.fori_loop(1, 64, sent, 0))
    for k in range(3):
        val = a1[k, coord[ORDERS[k][1]]].astype(F32)
        for o in range(3):
            val = val + r2[k, o].astype(F32)
        a2[k] = val.astype(BF16)
    stage(2, a2, r3)
    for k in range(3):
        val = a2[k, coord[ORDERS[k][2]]].astype(F32)
        for o in range(3):
            val = val + r3[k, o].astype(F32)
        out[48 * k : 48 * (k + 1), :] = val
    for q in writes:
        q.wait()


def layer(*args):
    vm = pl.BlockSpec(memory_space=pltpu.VMEM)
    sm = pl.BlockSpec(memory_space=pltpu.SMEM)
    hbm = pl.BlockSpec(memory_space=pl.ANY)
    dma = pltpu.SemaphoreType.DMA
    half = args[-1].shape[0]

    def room(*shape, dtype=BF16):
        return pltpu.VMEM(shape, dtype)

    return pl.pallas_call(
        layer_kernel,
        out_shape=(
            jax.ShapeDtypeStruct((32, 2048), BF16),
            jax.ShapeDtypeStruct((256, 256), BF16),
            jax.ShapeDtypeStruct((256, 128), BF16),
            jax.ShapeDtypeStruct((144, 128), F32),
        ),
        in_specs=[sm] + [hbm] * 14,
        out_specs=(hbm, hbm, hbm, vm),
        scratch_shapes=[
            room(6, 32, dtype=jnp.int32), room(6, 32, dtype=F32), room(32, 2048), room(32, 2048),
            room(64, 256), room(256, 256), room(256, 128), room(256, 2048),
            room(32, 2048), room(256, 256), room(256, 128),
            room(64, 8, 3072), room(64, 8, 3072),
            room(2, half, 2048), room(2, half, 2048), room(2, half, 2048),
            room(64, 8, 1536), room(64, 8, 1536),
            room(4, 4, 2, 2, 64, 640), room(4, 2, 32, 2048), room(4, 512, 32),
            room(192, 2048), room(192, 2048), room(2, 512, 2048, dtype=F32),
            room(512, 512), room(2, 256, 256), room(2, 256, 256), room(CHUNK, 512),
            room(2, 4, 4, 4, 144, 128), room(4, 4, 4, 144, 128),
            room(2, 3, 4, 4, 48, 128), room(3, 4, 4, 48, 128),
            room(3, 4, 4, 48, 128), room(3, 3, 4, 48, 128),
            room(3, 4, 48, 128), room(3, 3, 48, 128),
            dma((12,)), dma((3,)), pltpu.SemaphoreType.REGULAR((2,)),
            dma((3,)), dma, dma((64,)), dma((64,)), dma((3,)), dma((3,)),
            dma((64,)), dma((64,)), dma((2, 2, 3)), dma((2, 2, 3)), dma((5,)), dma((5,)), dma((4,)), dma((4,)),
            dma((4,)), dma((4,)), dma((2, 3, 4)), dma((2, 3, 4)), dma((3,)), dma((3,)),
            dma((2, 3, 3)), dma((2, 3, 3)),
        ],
        compiler_params=pltpu.CompilerParams(
            collective_id=0, has_side_effects=True, vmem_limit_bytes=67043328
        ),
        cost_estimate=pl.CostEstimate(flops=22 * 10**9, bytes_accessed=20 * 10**6, transcendentals=3 * 10**6),
    )(*args)


def lay_kernel(own, dq, dp, sums, own_out, dq_out, dp_out, lat_out, rope_out):
    own_out[...] = own[...]
    dq_out[...] = dq[...]
    dp_out[...] = dp[...]
    for l in range(4):
        lat_out[:, 128 * l : 128 * (l + 1)] = sums[32 * l : 32 * (l + 1), :]
    rope_out[0:16, :] = sums[128:144, 0:64]
    rope_out[16:32, :] = sums[128:144, 64:128]


def lay_out(*args):
    vm = pl.BlockSpec(memory_space=pltpu.VMEM)
    return pl.pallas_call(
        lay_kernel,
        out_shape=(
            jax.ShapeDtypeStruct((32, 2048), BF16),
            jax.ShapeDtypeStruct((256, 256), BF16),
            jax.ShapeDtypeStruct((256, 128), BF16),
            jax.ShapeDtypeStruct((32, 512), F32),
            jax.ShapeDtypeStruct((32, 64), F32),
        ),
        in_specs=[vm] * 4,
        out_specs=(vm,) * 5,
    )(*args)


def on_device(
    hidden, cotangent, routes, gates, offsets, w_gate, w_up, w_down, w_out,
    latent, rope_key, q_nope, q_pe, w_uk, w_uv,
):
    return lay_out(
        *layer(
            offsets, routes.T, gates.T, hidden, cotangent, latent, rope_key.T, q_nope, q_pe,
            w_uv, w_uk, w_out, w_gate[0].T, w_up[0].T, w_down[0],
        )
    )


def solution(mesh):
    both = ("wide", "narrow")
    return jax.shard_map(
        on_device,
        mesh=mesh,
        in_specs=(
            P(both, None), P(both, None), P(both, None), P(both, None), P(),
            P(both, None, None), P(both, None, None), P(both, None, None),
            P("narrow", None), P("wide", None), P("wide", None),
            P("wide", "narrow"), P("wide", "narrow"), P("narrow", None), P("narrow", None),
        ),
        out_specs=(
            P(both, None), P("wide", "narrow"), P("wide", "narrow"), P(both, None), P(both, None),
        ),
        check_vma=False,
    )
```

```python
import functools
import math

import jax
import jax.numpy as jnp
from jax import lax
from jax.experimental import pallas as pl
from jax.experimental.pallas import tpu as pltpu
from jax.sharding import PartitionSpec as P

LATENT = 512
NOPE = 128
ROPE = 64
VDIM = 128
MESH = pl.DeviceIdType.MESH
F32 = jnp.float32
BF16 = jnp.bfloat16
NT = (((1,), (1,)), ((), ()))
NN = (((1,), (0,)), ((), ()))
TN = (((0,), (0,)), ((), ()))


def dot(a, b, dims=NN):
    return lax.dot_general(a, b, dims, preferred_element_type=F32)


def iota(shape, dim):
    return lax.broadcasted_iota(jnp.int32, shape, dim)


def place():
    w = lax.axis_index("wide")
    n = lax.axis_index("narrow")
    return w // 4, w % 4, n // 2, n % 2


def selections(rt, gt):
    expert = iota((512, 32), 0) >> 3
    named = jnp.zeros((512, 32), F32)
    weight = jnp.zeros((512, 32), F32)
    for k in range(6):
        hit = expert == rt[k : k + 1, :]
        named = jnp.where(hit, 1.0, named)
        weight = jnp.where(hit, gt[k : k + 1, :], weight)
    earlier = (iota((32, 32), 0) < iota((32, 32), 1)).astype(F32).astype(BF16)
    before = dot(named.astype(BF16), earlier)
    row = iota((512, 32), 0) & 7
    picks = []
    for j in range(3):
        slot = jnp.where(row < 6, row, jnp.where(row == 6, j, 3 + j))
        picks.append(jnp.where(before == slot.astype(F32), named, 0.0))
    return picks, weight, row


def pack_matrix(j):
    q = iota((192, 256), 1)
    r = iota((192, 256), 0)
    s = q & 7
    base = (q >> 3) * 6
    if j < 0:
        return ((s < 6) & (r == base + s)).astype(F32).astype(BF16)
    return ((s >= 6) & (r == base + (s - 6) * 3 + j)).astype(F32).astype(BF16)


def fold_matrix(j):
    q = iota((256, 192), 0)
    r = iota((256, 192), 1)
    s = q & 7
    base = (q >> 3) * 6
    if j < 0:
        return ((s < 6) & (r == base + s)).astype(F32).astype(BF16)
    return ((s >= 6) & (r == base + (s - 6) * 3 + j)).astype(F32).astype(BF16)


ORDERS = ((2, 0, 1), (0, 1, 2), (1, 2, 0))
CHUNK = 512
CHUNKS = 8
SCALE = 1.0 / math.sqrt(NOPE + ROPE)


def layer_kernel(
    offs, rt_h, gt_h, hid_h, cot_h, lat_h, rope_h, qn_h, qp_h, wuv_h, wuk_h, wout_h, wg, wu, wd,
    own_h, dq_h, dp_h, out,
    rt, gt, hid, cot, rope, qn, qp, wout, own_out, dq_out, dp_out,
    send, recv, wgb, wub, wdb, back, landed, keys, gathered, comb, xs, dys, sc,
    wkv, qc, gx, dd, terms, r0, r1, ry, a1, r2, a2, r3,
    fsem, osem, sync, lsem, psem, ssem, rsem, wssem, wrsem, bssem, brsem, asem, bsem, gsem, hsem, psem2, qsem2,
    s0, t0, s1, t1, sy, ty, ss, rs,
):
    y, x, z, c = place()
    coord = (y, x, z)
    me = (y * 4 + x) * 4 + z
    partner = (y * 4 + x, z * 2 + 1 - c)

    def peer(k, sign=1):
        k = (k * 11) % 64
        pw = ((y + 4 + sign * (k // 16)) % 4) * 4 + (x + 4 + sign * ((k // 4) % 4)) % 4
        pz = (z + 4 + sign * (k % 4)) % 4
        return pw * 4 + pz, (pw, pz * 2 + c)

    def device(d, o):
        at = list(coord)
        at[d] = (at[d] + o) % 4
        return (at[0] * 4 + at[1], at[2] * 2 + c)

    def remote(src, dst, a, b, dev):
        return pltpu.make_async_remote_copy(
            src_ref=src, dst_ref=dst, send_sem=a, recv_sem=b, device_id=dev, device_id_type=MESH
        )

    bar = pltpu.get_barrier_semaphore()

    pl.semaphore_signal(bar, inc=1, device_id=partner, device_id_type=MESH)
    for d in range(3):
        for o in range(1, 4):
            pl.semaphore_signal(bar, inc=1, device_id=device(d, o), device_id_type=MESH)
    fetches = [
        (rt_h, rt), (gt_h, gt), (hid_h, hid), (cot_h, cot), (rope_h, rope),
        (lat_h.at[pl.ds(128 * c, 64)], keys.at[y, x, c, 0, :, pl.ds(0, 512)]),
        (lat_h.at[pl.ds(128 * c + 64, 64)], keys.at[y, x, c, 1, :, pl.ds(0, 512)]),
        (qn_h, qn), (qp_h, qp), (wuv_h, wkv.at[pl.ds(0, 256)]), (wuk_h, wkv.at[pl.ds(256, 256)]),
        (wout_h, wout),
    ]
    fetches = [pltpu.make_async_copy(a, b, fsem.at[i]) for i, (a, b) in enumerate(fetches)]
    for q in fetches:
        q.start()
    weights = ((wg, wgb), (wu, wub), (wd, wdb))
    loads = [pltpu.make_async_copy(a, b.at[0], lsem.at[i]) for i, (a, b) in enumerate(weights)]
    for q in loads:
        q.start()
    for q in fetches[:7]:
        q.wait()
    eye = (iota((64, 128), 0) == iota((64, 128), 1)).astype(F32).astype(BF16)
    turned = dot(rope[...], eye, TN).astype(BF16).reshape(2, 2, 64, 128)
    for h in range(2):

        @pl.when(c == h)
        def _(h=h):
            keys[y, x, h, :, :, 512:640] = turned[h]

    pl.semaphore_wait(bar, 10)
    spread = []
    for k, d in ((0, 1), (1, 0)):
        for o in range(1, 4):
            at = keys.at[y, x, c, k]
            spread.append(remote(at, at, asem.at[0, k, o - 1], bsem.at[0, k, o - 1], device(d, o)))
    for q in spread:
        q.start()
    for o in range(1, 4):
        pl.semaphore_signal(sync.at[0], inc=1, device_id=device(0, o), device_id_type=MESH)

    picks, weight, row = selections(rt[...], gt[...])
    cot_hi = cot[:, 1024:2048]
    for j in range(3):
        if j == 1:
            pl.semaphore_wait(sync.at[0], 3)
            for o in range(1, 4):
                pl.semaphore_signal(sync.at[1], inc=1, device_id=device(2, o), device_id_type=MESH)
        low = jnp.where(row < 6, picks[j], 0.0).astype(BF16)
        high = jnp.where(row < 6, 0.0, picks[j]).astype(BF16)
        if j == 0:
            comb[0] = low
        comb[1 + j] = high
        part = (hid[:, 0:1024], hid[:, 1024:2048], cot[:, 0:1024])[j]
        gate = jnp.sum(picks[j] * weight, axis=1, keepdims=True)
        if j < 2:
            gate = jnp.where(row[:, 0:1] < 6, 1.0, gate)
        val = (dot(low, part) + dot(high, cot_hi)) * gate
        send[:, :, 1024 * j : 1024 * (j + 1)] = val.astype(BF16).reshape(64, 8, 1024)
    zero = jnp.zeros((256, 64), BF16)
    pl.semaphore_wait(sync.at[1], 3)

    def start(k, _):
        pc, dev = peer(k)
        remote(send.at[pc], recv.at[k], ssem.at[k], rsem.at[k], dev).start()
        return 0

    trades = [
        remote(a, b.at[1], wssem.at[i], wrsem.at[i], partner) for i, (a, b) in enumerate(weights)
    ]
    own = pltpu.make_async_copy(send.at[me], recv.at[0], psem)
    own.start()
    lax.fori_loop(1, 64, start, 0, unroll=3)
    for q in trades:
        q.start()
    for q in fetches[7:]:
        q.wait()
    for h in range(2):
        qc[h, :, 0:128] = qn[:, 128 * h : 128 * (h + 1)]
        qc[h, :, 128:256] = jnp.concatenate([qp[:, 64 * h : 64 * (h + 1)], zero], axis=1)
    own.wait()

    def arrive(k, _):
        remote(send.at[0], recv.at[k], ssem.at[k], rsem.at[k], partner).wait_recv()
        return 0

    def ret_start(k, _):
        remote(back.at[k], landed.at[me], bssem.at[k], brsem.at[me], peer(k, -1)[1]).start()
        return 0

    widen = []
    for k, d in ((0, 0), (1, 1)):
        for o in range(1, 4):
            at = keys.at[y, :, c, 0] if k == 0 else keys.at[:, x, c, 1]
            widen.append(remote(at, at, asem.at[1, k, o - 1], bsem.at[1, k, o - 1], device(d, o)))
    mirror = remote(keys.at[:, :, c], keys.at[:, :, c], gsem.at[4], hsem.at[4], partner)

    for g in range(2):
        lax.fori_loop(max(1, 32 * g), 32 * (g + 1), arrive, 0)
        plain = pack_matrix(-1)

        def cols(a, b, g=g):
            return recv[32 * g : 32 * (g + 1), :, a:b].reshape(256, b - a)

        xs[:, 0:1024] = dot(plain, cols(0, 1024)).astype(BF16)
        xs[:, 1024:2048] = dot(plain, cols(1024, 2048)).astype(BF16)
        dys[:, 0:1024] = dot(plain, cols(2048, 3072)).astype(BF16)
        hi = dot(pack_matrix(0), cols(0, 1024))
        hi = hi + dot(pack_matrix(1), cols(1024, 2048))
        hi = hi + dot(pack_matrix(2), cols(2048, 3072))
        dys[:, 1024:2048] = hi.astype(BF16)
        if g == 0:
            for q in loads:
                q.wait()
        for h in range(2):
            if g == 0 and h == 1:
                for q in trades:
                    q.wait()
            if g == 1 and h == 1:
                for q in widen:
                    q.wait()
                mirror.start()
            pre = dot(xs[...], wgb[h], NT)
            up = dot(xs[...], wub[h], NT)
            gh = dot(dys[...], wdb[h], NT)
            s = jax.nn.sigmoid(pre)
            gg = (gh * up * s * (1.0 + pre * (1.0 - s))).astype(BF16)
            gu = (gh * pre * s).astype(BF16)
            for b in range(2):
                cs = slice(1024 * b, 1024 * (b + 1))
                term = dot(gg, wgb[h, :, cs]) + dot(gu, wub[h, :, cs])
                if h == 0:
                    sc[0, 0:192, cs] = term
                else:
                    xs[:, cs] = (sc[0, 0:192, cs] + term).astype(BF16)
        plain = fold_matrix(-1)
        for j in range(3):
            val = dot(plain, xs[:, 512 * j : 512 * (j + 1)])
            val = val + dot(fold_matrix(j), xs[:, 1536:2048])
            back[32 * g : 32 * (g + 1), :, 512 * j : 512 * (j + 1)] = val.astype(BF16).reshape(32, 8, 512)
        if g == 0:
            for q in spread:
                q.wait()
            for q in widen:
                q.start()
            own = pltpu.make_async_copy(back.at[0], landed.at[me], psem)
            own.start()
        lax.fori_loop(max(1, 32 * g), 32 * (g + 1), ret_start, 0)

    mirror.wait()
    ones = (iota((CHUNK, 128), 1) < 2).astype(F32).astype(BF16)
    delta = iota((256, 256), 0) - iota((256, 256), 1)
    here = offs[y * 4 + x]

    def block(i):
        return slice(0, CHUNK), pl.ds(pl.multiple_of(i * 256, 256), 256)

    def forward(i, tops):
        sub, at = block(i)
        chunk = keys[i // 2, pl.ds((i % 2) * 2, 2)].reshape(CHUNK, 640)
        kv = dot(chunk[:, 0:512], wkv[...], NT).astype(BF16)
        new = []
        for h in range(2):
            vx = jnp.concatenate([kv[:, 128 * h : 128 * (h + 1)], ones], axis=1)
            kc = jnp.concatenate([kv[:, 256 + 128 * h : 256 + 128 * (h + 1)], chunk[:, 512:640]], axis=1)
            wdb[h, sub, at] = vx
            wub[h, sub, at] = kc
            top = tops[h]
            val = dot(kc, qc[h], NT)
            for b in range(2):
                limit = (here - offs[2 * i + b]) * 256
                part = jnp.where(delta <= limit, val[256 * b : 256 * (b + 1)], -1e30)
                sc[h, 256 * b : 256 * (b + 1), at] = part
                top = jnp.maximum(top, jnp.max(part.reshape(32, 8, 256), axis=0))
            new.append(top)
        return tuple(new)

    least = jnp.full((8, 256), -1e30, F32)
    tops = lax.fori_loop(0, CHUNKS, forward, (least, least))
    tops = [jnp.max(t, axis=0, keepdims=True) for t in tops]

    def weigh(i, sums):
        sub, at = block(i)
        new = []
        for h in range(2):
            p = jnp.exp(SCALE * (sc[h, sub, at] - tops[h])).astype(BF16)
            wgb[h, sub, at] = p
            new.append(sums[h] + dot(p, wdb[h, sub, at], TN))
        return tuple(new)

    nil = jnp.zeros((256, 256), F32)
    sums = lax.fori_loop(0, CHUNKS, weigh, (nil, nil))

    own.wait()

    def ret_finish(k, _):
        pc = (me + k) % 64
        remote(back.at[k], landed.at[pc], bssem.at[k], brsem.at[pc], partner).wait_recv()
        return 0

    def sent(k, _):
        remote(send.at[0], recv.at[k], ssem.at[k], rsem.at[k], partner).wait_send()
        remote(back.at[k], landed.at[me], bssem.at[k], brsem.at[me], partner).wait_send()
        return 0

    lax.fori_loop(1, 64, ret_finish, 0, unroll=3)

    total = cot[...].astype(F32)
    rest = jnp.zeros((32, 512), F32)
    for j in range(3):
        part = landed[:, :, 512 * j : 512 * (j + 1)].reshape(512, 512)
        cs = slice(512 * j, 512 * (j + 1))
        own_out[:, cs] = (total[:, cs] + dot(comb[0], part, TN)).astype(BF16)
        rest = rest + dot(comb[1 + j], part, TN)
    own_out[:, 1536:2048] = (total[:, 1536:2048] + rest).astype(BF16)
    gathered[z, c] = own_out[...]
    writes = [
        pltpu.make_async_copy(a, b, osem.at[i])
        for i, (a, b) in enumerate(((own_out, own_h), (dq_out, dq_h), (dp_out, dp_h)))
    ]
    writes[0].start()
    hops = [
        remote(own_out, gathered.at[z, c], gsem.at[o - 1], hsem.at[o - 1], device(2, o))
        for o in range(1, 4)
    ]
    for q in hops:
        q.start()

    def pair(o):
        at = gathered.at[(z + 4 - o) % 4, c]
        return remote(at, at, psem2.at[o], qsem2.at[o], partner)

    pair(0).start()
    for o in range(1, 4):
        hops[o - 1].wait()
        pair(o).start()
    for o in range(4):
        pair(o).wait()

    go = dot(gathered[...].reshape(256, 2048), wout[...], NT).astype(BF16).astype(F32)
    lane = iota((256, 128), 1)
    for h in range(2):
        inv = 1.0 / sums[h][:, 128:129]
        mean = sums[h][:, 0:128] * inv
        scaled = (go[:, 128 * h : 128 * (h + 1)] * inv).astype(BF16)
        drop = -jnp.sum(scaled.astype(F32) * mean, axis=1, keepdims=True)
        high = drop.astype(BF16).astype(F32)
        extra = jnp.where(lane == 0, high, jnp.where(lane == 1, drop - high, 0.0))
        gx[h, :, 0:128] = scaled
        gx[h, :, 128:256] = extra.astype(BF16)

    def trade(r):
        g = (y + 1 + r) % 4
        return remote(terms.at[1 - c, g], r0.at[g], s0.at[r], t0.at[r], partner)

    left = iota((16, 128), 1) < 64

    def backward(i, dqs):
        sub, at = block(i)
        new = []
        ropes = 0.0
        for h in range(2):
            p = wgb[h, sub, at]
            diff = dot(wdb[h, sub, at], gx[h], NT)
            ds = (p.astype(F32) * diff).astype(BF16)
            new.append(dqs[h] + dot(ds, wub[h, sub, at], TN))
            dk = dot(ds, qc[h]) * SCALE
            dd[:, 128 * h : 128 * (h + 1)] = dot(p, gx[h, :, 0:128]).astype(BF16)
            dd[:, 256 + 128 * h : 256 + 128 * (h + 1)] = dk[:, 0:128].astype(BF16)
            ropes = ropes + dk[:, 128:256]
        turned = pltpu.roll(ropes, 64, 1)
        tl = dot(dd[...], wkv[...]).astype(BF16)
        for q in range(16):
            e, f, m = i // 2, (i % 2) * 2 + q // 8, (q // 2) % 4
            for l in range(4):
                terms[q % 2, e, f, m, 32 * l : 32 * (l + 1), :] = tl[32 * q : 32 * (q + 1), 128 * l : 128 * (l + 1)]
            terms[q % 2, e, f, m, 128:144, :] = jnp.where(
                left, ropes[32 * q : 32 * q + 16], turned[32 * q + 16 : 32 * q + 32]
            ).astype(BF16)
        return tuple(new)

    def near(r, k, o):
        g = (y + 1 + r) % 4
        d = ORDERS[k][0]
        rows = pl.ds(48 * k, 48)
        to = (coord[d] + o) % 4
        src = terms.at[c, g, :, to, rows] if k == 0 else terms.at[c, g, to, :, rows]
        i = k // 2
        return remote(src, r1.at[i, o - 1, g], s1.at[i, o - 1, r], t1.at[i, o - 1, r], device(d, o))

    def far(r):
        g = (y + 1 + r) % 4
        pz = z * 2 + c
        return remote(terms.at[c, g, :, :, pl.ds(48, 48)], ry.at[r], sy.at[r], ty.at[r], (g * 4 + x, pz))

    def settle(r):
        trade(r).wait()
        g = (y + 1 + r) % 4

        def add(i, _):
            a, b = i // 4, i % 4
            val = terms[c, g, a, b].astype(F32) + r0[g, a, b].astype(F32)
            terms[c, g, a, b] = val.astype(BF16)
            return 0

        lax.fori_loop(0, 16, add, 0)
        for o in range(1, 4):
            near(r, 0, o).start()
            near(r, 2, o).start()

        @pl.when(r < 3)
        def _():
            far(r).start()

    def quarter(r, dqs):
        i = ((y + 1 + r) % 4) * 2
        dqs = lax.fori_loop(i, i + 2, backward, dqs)
        trade(r).start()

        @pl.when(r > 0)
        def _():
            settle(r - 1)

        return dqs

    dqs = lax.fori_loop(0, 4, quarter, (nil, nil))
    for h in range(2):
        val = (dqs[h] * SCALE).astype(BF16)
        dq_out[:, 128 * h : 128 * (h + 1)] = val[:, 0:128]
        dp_out[:, 64 * h : 64 * (h + 1)] = val[:, 128:192]
    writes[1].start()
    writes[2].start()
    settle(3)

    def close(r, _):
        for o in range(1, 4):
            near(r, 0, o).wait()
            near(r, 2, o).wait()

        @pl.when(r < 3)
        def _():
            far(r).wait()

        return 0

    lax.fori_loop(0, 4, close, 0)

    def add1(i, _):
        a, b = i // 4, i % 4
        val = terms[c, a, b, z, 0:48].astype(F32)
        for o in range(3):
            val = val + r1[0, o, a, b].astype(F32)
        a1[0, a, b] = val.astype(BF16)
        val = terms[c, y, a, b, 48:96].astype(F32)
        for o in range(3):
            val = val + ry[o, a, b].astype(F32)
        a1[1, a, b] = val.astype(BF16)
        val = terms[c, a, x, b, 96:144].astype(F32)
        for o in range(3):
            val = val + r1[1, o, a, b].astype(F32)
        a1[2, b, a] = val.astype(BF16)
        return 0

    lax.fori_loop(0, 16, add1, 0)

    def stage(i, src, dst, beside=None):
        copies = []
        for o in range(1, 4):
            for k in range(3):
                d = ORDERS[k][i]
                copies.append(
                    remote(
                        src.at[k, (coord[d] + o) % 4], dst.at[k, o - 1],
                        ss.at[i - 1, k, o - 1], rs.at[i - 1, k, o - 1], device(d, o),
                    )
                )
        for q in copies:
            q.start()
        if beside:
            beside()
        for q in copies:
            q.wait()

    stage(1, a1, r2, lambda: lax.fori_loop(1, 64, sent, 0))
    for k in range(3):
        val = a1[k, coord[ORDERS[k][1]]].astype(F32)
        for o in range(3):
            val = val + r2[k, o].astype(F32)
        a2[k] = val.astype(BF16)
    stage(2, a2, r3)
    for k in range(3):
        val = a2[k, coord[ORDERS[k][2]]].astype(F32)
        for o in range(3):
            val = val + r3[k, o].astype(F32)
        out[48 * k : 48 * (k + 1), :] = val
    for q in writes:
        q.wait()


def layer(*args):
    vm = pl.BlockSpec(memory_space=pltpu.VMEM)
    sm = pl.BlockSpec(memory_space=pltpu.SMEM)
    hbm = pl.BlockSpec(memory_space=pl.ANY)
    dma = pltpu.SemaphoreType.DMA
    half = args[-1].shape[0]

    def room(*shape, dtype=BF16):
        return pltpu.VMEM(shape, dtype)

    return pl.pallas_call(
        layer_kernel,
        out_shape=(
            jax.ShapeDtypeStruct((32, 2048), BF16),
            jax.ShapeDtypeStruct((256, 256), BF16),
            jax.ShapeDtypeStruct((256, 128), BF16),
            jax.ShapeDtypeStruct((144, 128), F32),
        ),
        in_specs=[sm] + [hbm] * 14,
        out_specs=(hbm, hbm, hbm, vm),
        scratch_shapes=[
            room(6, 32, dtype=jnp.int32), room(6, 32, dtype=F32), room(32, 2048), room(32, 2048),
            room(64, 256), room(256, 256), room(256, 128), room(256, 2048),
            room(32, 2048), room(256, 256), room(256, 128),
            room(64, 8, 3072), room(64, 8, 3072),
            room(2, half, 2048), room(2, half, 2048), room(2, half, 2048),
            room(64, 8, 1536), room(64, 8, 1536),
            room(4, 4, 2, 2, 64, 640), room(4, 2, 32, 2048), room(4, 512, 32),
            room(192, 2048), room(192, 2048), room(2, 512, 2048, dtype=F32),
            room(512, 512), room(2, 256, 256), room(2, 256, 256), room(CHUNK, 512),
            room(2, 4, 4, 4, 144, 128), room(4, 4, 4, 144, 128),
            room(2, 3, 4, 4, 48, 128), room(3, 4, 4, 48, 128),
            room(3, 4, 4, 48, 128), room(3, 3, 4, 48, 128),
            room(3, 4, 48, 128), room(3, 3, 48, 128),
            dma((12,)), dma((3,)), pltpu.SemaphoreType.REGULAR((2,)),
            dma((3,)), dma, dma((64,)), dma((64,)), dma((3,)), dma((3,)),
            dma((64,)), dma((64,)), dma((2, 2, 3)), dma((2, 2, 3)), dma((5,)), dma((5,)), dma((4,)), dma((4,)),
            dma((4,)), dma((4,)), dma((2, 3, 4)), dma((2, 3, 4)), dma((3,)), dma((3,)),
            dma((2, 3, 3)), dma((2, 3, 3)),
        ],
        compiler_params=pltpu.CompilerParams(
            collective_id=0, has_side_effects=True, vmem_limit_bytes=67043328
        ),
        cost_estimate=pl.CostEstimate(flops=22 * 10**9, bytes_accessed=20 * 10**6, transcendentals=3 * 10**6),
    )(*args)


def lay_kernel(own, dq, dp, sums, own_out, dq_out, dp_out, lat_out, rope_out):
    own_out[...] = own[...]
    dq_out[...] = dq[...]
    dp_out[...] = dp[...]
    for l in range(4):
        lat_out[:, 128 * l : 128 * (l + 1)] = sums[32 * l : 32 * (l + 1), :]
    rope_out[0:16, :] = sums[128:144, 0:64]
    rope_out[16:32, :] = sums[128:144, 64:128]


def lay_out(*args):
    vm = pl.BlockSpec(memory_space=pltpu.VMEM)
    return pl.pallas_call(
        lay_kernel,
        out_shape=(
            jax.ShapeDtypeStruct((32, 2048), BF16),
            jax.ShapeDtypeStruct((256, 256), BF16),
            jax.ShapeDtypeStruct((256, 128), BF16),
            jax.ShapeDtypeStruct((32, 512), F32),
            jax.ShapeDtypeStruct((32, 64), F32),
        ),
        in_specs=[vm] * 4,
        out_specs=(vm,) * 5,
    )(*args)


def on_device(
    hidden, cotangent, routes, gates, offsets, w_gate, w_up, w_down, w_out,
    latent, rope_key, q_nope, q_pe, w_uk, w_uv,
):
    return lay_out(
        *layer(
            offsets, routes.T, gates.T, hidden, cotangent, latent, rope_key.T, q_nope, q_pe,
            w_uv, w_uk, w_out, w_gate[0].T, w_up[0].T, w_down[0],
        )
    )


def solution(mesh):
    both = ("wide", "narrow")
    return jax.shard_map(
        on_device,
        mesh=mesh,
        in_specs=(
            P(both, None), P(both, None), P(both, None), P(both, None), P(),
            P(both, None, None), P(both, None, None), P(both, None, None),
            P("narrow", None), P("wide", None), P("wide", None),
            P("wide", "narrow"), P("wide", "narrow"), P("narrow", None), P("narrow", None),
        ),
        out_specs=(
            P(both, None), P("wide", "narrow"), P("wide", "narrow"), P(both, None), P(both, None),
        ),
        check_vma=False,
    )
```
